256 devices in a mesh: gx: 16 (over z_lo, x), gy: 8 (over y, z_hi), gz: 2 (over core).
Axes of the slice: x: 4, y: 4, z: 8 (z_hi: 2, z_lo: 4; z = z_hi * 4 + z_lo), core: 2. Of those that a mesh axis runs over, the one named last changes fastest.
Arguments:
- pressure: float32 [128, 256, 256], P('gx', 'gy', 'gz'), may hold values from -6 to 6
- accumulation: float32 [128, 256, 256], P('gx', 'gy', 'gz'), may hold values from 0.05 to 0.5
- trans_x: float32 [128, 256, 256], P('gx', 'gy', 'gz'), may hold values from 0.1 to 1
- trans_y: float32 [128, 256, 256], P('gx', 'gy', 'gz'), may hold values from 0.1 to 1
- trans_z: float32 [128, 256, 256], P('gx', 'gy', 'gz'), may hold values from 0.1 to 1
- source: float32 [128, 256, 256], P('gx', 'gy', 'gz'), may hold values from -6 to 6
- well_cells: int32 [1024], replicated, may hold values from 0 to 8388607
- well_rates: float32 [1024], replicated, may hold values from -16 to 16
- basis: bfloat16 [6, 12, 12, 16, 32, 64], P(None, None, None, 'gx', 'gy', 'gz'), may hold values from 0 to 0.099609375
- coarse_off: float32 [26, 16, 32, 64], P(None, 'gx', 'gy', 'gz'), may hold values from -0.1 to -0.02
- coarse_diag: float32 [16, 32, 64], P('gx', 'gy', 'gz'), may hold values from 3 to 6
Outputs:
- residual: float32 [128, 256, 256], P('gx', 'gy', 'gz')
- coarse_solution: float32 [16, 32, 64], P('gx', 'gy', 'gz')
- new_pressure: float32 [128, 256, 256], P('gx', 'gy', 'gz')
The draws below stay inside these ranges and needn't reach their ends.
All inputs are finite; a program needn't handle non-finite values.
Results may differ from the reference program's by a relative error of at most 0.0004.
Values may be sent and summed in bfloat16 or wider, within the bound.
No kernel may reach another device: no remote copies, remote signals or barrier semaphores. Data moves between devices by JAX's collectives and lax.ppermute only.
A program may use at most 128 MiB of HBM per device.

```python
import math
import jax
import jax.numpy as jnp
from jax import lax

BLOCK_XY = 8
BLOCK_Z = 4
SPAN_XY = 12
SPAN_Z = 6
ITERS = 4
WELLS = 1024
NX = 128
NY = 256
NZ = 256
NBX = 16
NBY = 32
NBZ = 64


def set_ends(entries, rng, smallest, largest):
    spot = [jax.random.randint(jax.random.fold_in(rng, axis), (), 0, length) for axis, length in enumerate(entries.shape)]
    longest = entries.shape.index(max(entries.shape))
    beside = spot[:longest] + [(spot[longest] + 1) % entries.shape[longest]] + spot[longest + 1:]
    return entries.at[tuple(spot)].set(smallest).at[tuple(beside)].set(largest)


def levels(key, extent, pieces, smallest, high):
    def one(dim, shards_of):
        steps = jax.random.uniform(jax.random.fold_in(jax.random.fold_in(key, 6), dim), (shards_of,), jnp.float32, smallest / len(pieces), high / len(pieces))
        return jnp.repeat(jnp.exp(steps), extent[dim] // shards_of).reshape((-1,) + (1,) * (len(extent) - dim - 1))

    gain = one(*pieces[0])
    for cut in pieces[1:]:
        gain = gain * one(*cut)
    return gain


def normal_values(own_key, dims, width, bound, split=(), held_as=jnp.bfloat16):
    drawn = width * jax.random.normal(own_key, dims, jnp.float32)
    if split:
        drawn = drawn * levels(own_key, dims, split, -0.22, 0.18)
    return jnp.clip(drawn, -bound, bound).astype(held_as)


def setup_inputs(seed: int = 0) -> dict:
    arg_keys = jax.random.split(jax.random.key(seed), 12)
    pressure = normal_values(arg_keys[0], (NX, NY, NZ), 1.0, 6.0, ((0, 16), (1, 8), (2, 2)), jnp.float32)
    accumulation = jnp.clip(jnp.exp(math.log(0.5) - 2.3025851 * jax.random.uniform(arg_keys[1], (NX, NY, NZ), jnp.float32) ** levels(arg_keys[1], (NX, NY, NZ), ((0, 16), (1, 8), (2, 2)), -0.2, 0.2)), 0.05, 0.5)
    trans_x = jnp.clip(jnp.exp(math.log(1.0) - 2.3025851 * jax.random.uniform(arg_keys[2], (NX, NY, NZ), jnp.float32) ** levels(arg_keys[2], (NX, NY, NZ), ((0, 16), (1, 8), (2, 2)), -0.2, 0.2)), 0.1, 1.0)
    trans_y = jnp.clip(jnp.exp(math.log(1.0) - 2.3025851 * jax.random.uniform(arg_keys[3], (NX, NY, NZ), jnp.float32) ** levels(arg_keys[3], (NX, NY, NZ), ((0, 16), (1, 8), (2, 2)), -0.2, 0.2)), 0.1, 1.0)
    trans_z = jnp.clip(jnp.exp(math.log(1.0) - 2.3025851 * jax.random.uniform(arg_keys[4], (NX, NY, NZ), jnp.float32) ** levels(arg_keys[4], (NX, NY, NZ), ((0, 16), (1, 8), (2, 2)), -0.2, 0.2)), 0.1, 1.0)
    source = normal_values(arg_keys[5], (NX, NY, NZ), 1.0, 6.0, ((0, 16), (1, 8), (2, 2)), jnp.float32)
    well_cells = set_ends(jax.random.randint(arg_keys[6], (WELLS,), 0, NX * NY * NZ), jax.random.fold_in(arg_keys[6], 1), 0, (NX * NY * NZ) - 1).astype(jnp.int32)
    well_rates = normal_values(arg_keys[7], (WELLS,), 4.0, 16.0, (), jnp.float32)
    basis = jnp.clip(0.099609375 * jax.random.uniform(arg_keys[8], (SPAN_Z, SPAN_XY, SPAN_XY, NBX, NBY, NBZ), jnp.float32) ** levels(arg_keys[8], (SPAN_Z, SPAN_XY, SPAN_XY, NBX, NBY, NBZ), ((3, 16), (4, 8), (5, 2)), -0.2, 0.2), 0.0, 0.099609375).astype(jnp.bfloat16)
    coarse_off = jnp.clip(-0.1 + 0.08 * jax.random.uniform(arg_keys[9], (26, NBX, NBY, NBZ), jnp.float32) ** levels(arg_keys[9], (26, NBX, NBY, NBZ), ((1, 16), (2, 8), (3, 2)), -0.2, 0.2), -0.1, -0.02)
    coarse_diag = jnp.clip(3.0 + 3.0 * jax.random.uniform(arg_keys[10], (NBX, NBY, NBZ), jnp.float32) ** levels(arg_keys[10], (NBX, NBY, NBZ), ((0, 16), (1, 8), (2, 2)), -0.2, 0.2), 3.0, 6.0)
    return dict(pressure=pressure, accumulation=accumulation, trans_x=trans_x, trans_y=trans_y, trans_z=trans_z, source=source, well_cells=well_cells, well_rates=well_rates, basis=basis, coarse_off=coarse_off, coarse_diag=coarse_diag)


damping = 0.8


def place(values, offset, length):
    padded = jnp.pad(values, [(offset, 0)] + [(0, 0)] * (values.ndim - 1))
    if padded.shape[0] >= length:
        return padded[:length]
    return jnp.pad(padded, [(0, length - padded.shape[0])] + [(0, 0)] * (values.ndim - 1))


def expand(field, axis, block, span, start, count):
    moved = jnp.moveaxis(field, axis, 0)
    others = moved.shape[1:]
    first = lax.slice_in_dim(moved, start, start + block * count, axis=0).reshape((count, block) + others)
    padded = jnp.pad(moved, [(0, 2 * block)] + [(0, 0)] * len(others))
    second = lax.slice_in_dim(padded, start + block, start + block + block * count, axis=0).reshape((count, block) + others)
    window = jnp.concatenate([first, second[:, : span - block]], axis=1)
    window = jnp.moveaxis(window, 1, 0)
    return jnp.moveaxis(window, 1, axis + 1)


def fold(window, axis, block, span, start, count, length):
    moved = jnp.moveaxis(window, axis + 1, 0)
    others = moved.shape[2:]
    first = moved[:, :block].reshape((count * block,) + others)
    second = jnp.pad(moved[:, block:], [(0, 0), (0, 2 * block - span)] + [(0, 0)] * len(others))
    second = second.reshape((count * block,) + others)
    total = place(first, start, length) + place(second, start + block, length)
    return jnp.moveaxis(total, 0, axis)


def offsets_list():
    result = []
    for first in (-1, 0, 1):
        for second in (-1, 0, 1):
            for third in (-1, 0, 1):
                if first != 0 or second != 0 or third != 0:
                    result.append((first, second, third))
    return result


def reference(pressure, accumulation, trans_x, trans_y, trans_z, source, well_cells, well_rates, basis, coarse_off, coarse_diag):
    wells = jnp.zeros((NX * NY * NZ,), jnp.float32).at[well_cells].add(well_rates).reshape(NX, NY, NZ)
    rhs = source + wells
    padded = jnp.pad(pressure, 1)
    tx_pad = jnp.pad(trans_x, 1)
    ty_pad = jnp.pad(trans_y, 1)
    tz_pad = jnp.pad(trans_z, 1)
    center = padded[1:-1, 1:-1, 1:-1]
    flux = trans_x * (center - padded[2:, 1:-1, 1:-1]) + tx_pad[:-2, 1:-1, 1:-1] * (center - padded[:-2, 1:-1, 1:-1])
    flux = flux + trans_y * (center - padded[1:-1, 2:, 1:-1]) + ty_pad[1:-1, :-2, 1:-1] * (center - padded[1:-1, :-2, 1:-1])
    flux = flux + trans_z * (center - padded[1:-1, 1:-1, 2:]) + tz_pad[1:-1, 1:-1, :-2] * (center - padded[1:-1, 1:-1, :-2])
    residual = rhs - accumulation * pressure - flux

    resid_pad = jnp.pad(residual, 2)

    def restrict_slab(index_x):
        slab = lax.dynamic_slice_in_dim(resid_pad, index_x * BLOCK_XY, SPAN_XY, 0)
        window = expand(slab, 1, BLOCK_XY, SPAN_XY, 0, NBY)
        window = expand(window, 3, BLOCK_Z, SPAN_Z, 1, NBZ)
        tile = lax.dynamic_index_in_dim(basis, index_x, 3, keepdims=False).astype(jnp.float32)
        return jnp.sum(tile * window, axis=(0, 1, 2))

    coarse_rhs = lax.map(restrict_slab, jnp.arange(NBX, dtype=jnp.int32))

    solution = jnp.zeros((NBX, NBY, NBZ), jnp.float32)
    for sweep_index in range(ITERS):
        sol_pad = jnp.pad(solution, 1)
        applied = coarse_diag * solution
        for number, (first, second, third) in enumerate(offsets_list()):
            applied = applied + coarse_off[number] * sol_pad[1 + first:1 + first + NBX, 1 + second:1 + second + NBY, 1 + third:1 + third + NBZ]
        solution = solution + damping * (coarse_rhs - applied) / coarse_diag

    canvas = jnp.zeros((BLOCK_XY * NBX + 4, BLOCK_XY * NBY + 4, BLOCK_Z * NBZ + 4), jnp.float32)

    def add_slab(current, index_x):
        tile = lax.dynamic_index_in_dim(basis, index_x, 3, keepdims=False).astype(jnp.float32)
        values = lax.dynamic_index_in_dim(solution, index_x, 0, keepdims=False)
        window = tile * values
        window = fold(window, 3, BLOCK_Z, SPAN_Z, 1, NBZ, BLOCK_Z * NBZ + 4)
        window = fold(window, 1, BLOCK_XY, SPAN_XY, 0, NBY, BLOCK_XY * NBY + 4)
        older = lax.dynamic_slice_in_dim(current, index_x * BLOCK_XY, SPAN_XY, 0)
        return lax.dynamic_update_slice_in_dim(current, older + window, index_x * BLOCK_XY, 0), None

    canvas, unused = lax.scan(add_slab, canvas, jnp.arange(NBX, dtype=jnp.int32))
    correction = canvas[2:-2, 2:-2, 2:-2]
    return residual, solution, pressure + correction
```

```python
import functools

import jax
import jax.numpy as jnp
from jax import lax
from jax.experimental import pallas as pl
from jax.experimental.pallas import tpu as pltpu
from jax.sharding import PartitionSpec as P

damping = 0.8
F32 = jnp.float32
BF16 = jnp.bfloat16


def iota(shape, dim):
    return lax.broadcasted_iota(jnp.int32, shape, dim)


def parts(a):
    high = a.astype(BF16)
    rest = a - high.astype(F32)
    middle = rest.astype(BF16)
    low = (rest - middle.astype(F32)).astype(BF16)
    return high, middle, low


NN = (((1,), (0,)), ((), ()))
NT = (((1,), (1,)), ((), ()))


def dot(a, b, dims=NN):
    return lax.dot_general(a, b, dims, preferred_element_type=F32)


def dot3(a, b, dims=NN):
    high, middle, low = parts(a)
    return dot(high, b, dims) + dot(middle, b, dims) + dot(low, b, dims)


def spread(core):
    lane = iota((128, 128), 0)
    block = iota((128, 128), 1)
    own = core * 32 + lane // 4
    inside = jnp.where(block == own, 1.0, 0.0).astype(BF16)
    below = (lane % 4 == 0) & (block == own - 1)
    above = (lane % 4 == 3) & (block == own + 1)
    reach = jnp.where(below | above, 1.0, 0.0) * jnp.where(block < 64, 1.0, 0.0)
    return inside, reach.astype(BF16)


def pack_kernel(basis, facing, pressure, trans_x, trans_y, coarse, wo, wz, to_next_x, to_prev_x, to_next_y, to_prev_y):
    core = lax.axis_index("gz")
    block = iota((32, 128), 0)
    lane = iota((32, 128), 1)

    def place(mask):
        return jnp.where(mask, 1.0, 0.0).astype(BF16)

    total = dot(basis[1], place(lane == 4 * block))
    for k in (2, 3, 4):
        total = total + dot(basis[k], place(lane == 4 * block + (k - 1)))
    wo[...] = total
    edge = ((block == 31) & (lane == 0) & (core == 1)) | ((block == 0) & (lane == 127) & (core == 0))
    wz[...] = (
        dot(basis[5], place(lane == 4 * block + 4))
        + dot(basis[0], place(lane == 4 * block - 1))
        + dot(facing[...], place(edge))
    )
    for j in range(12):
        to_next_x[pl.ds(8 * j, 8), :] = wo[pl.ds(48 * j + 40, 8), :]
        to_next_x[pl.ds(96 + 8 * j, 8), :] = wz[pl.ds(48 * j + 40, 8), :]
        to_prev_x[pl.ds(8 * j, 8), :] = wo[pl.ds(48 * j, 8), :]
        to_prev_x[pl.ds(96 + 8 * j, 8), :] = wz[pl.ds(48 * j, 8), :]
    to_next_x[pl.ds(192, 32), :] = pressure[7]
    to_next_x[pl.ds(224, 32), :] = trans_x[7]
    to_prev_x[pl.ds(192, 32), :] = pressure[0]
    for n in range(2):
        for half, w in enumerate((wo, wz)):
            spot = (2 * n + half) * 12
            to_next_y[pl.ds(spot, 12), :] = w[pl.ds((10 + n) * 48 + 3, 12, stride=4), :]
            to_prev_y[pl.ds(spot, 12), :] = w[pl.ds(n * 48, 12, stride=4), :]
    for x in range(8):
        to_next_y[pl.ds(48 + x, 1), :] = pressure[x, pl.ds(31, 1), :]
        to_next_y[pl.ds(56 + x, 1), :] = trans_y[x, pl.ds(31, 1), :]
        to_prev_y[pl.ds(48 + x, 1), :] = pressure[x, pl.ds(0, 1), :]
    to_next_y[pl.ds(64, 32), :] = coarse[...]
    to_prev_y[pl.ds(56, 32), :] = coarse[...]


def restrict_kernel(
    pressure, accumulation, trans_x, trans_y, trans_z, source, cells, rates, facing_p, facing_t, wo, wz,
    from_prev_x, from_next_x, from_prev_y, from_next_y, corner_prev, corner_next, coarse,
    residual, box, field, sums_o, sums_z,
):
    gx = lax.axis_index("gx")
    gy = lax.axis_index("gy")
    core = lax.axis_index("gz")
    size_x = lax.axis_size("gx")
    size_y = lax.axis_size("gy")

    rows_at = iota((256, 128), 0)
    lane_at = iota((128, 128), 0)
    wells = jnp.zeros((256, 128), F32)
    for c in range(8):
        cell = cells[pl.ds(c, 1), :]
        at_x = (cell >> 16) - gx * 8
        at_y = ((cell >> 8) & 255) - gy * 32
        at_z = (cell & 255) - core * 128
        inside = (at_x >= 0) & (at_x < 8) & (at_y >= 0) & (at_y < 32)
        row = jnp.where(inside, at_x * 32 + at_y, -1)
        hit = jnp.where(row == rows_at, 1.0, 0.0).astype(BF16)
        rate = rates[pl.ds(c, 1), :]
        high, middle, low = parts(rate)
        here = at_z == lane_at
        for part in (high, middle, low):
            wells = wells + dot(hit, jnp.where(here, part.astype(F32), 0.0).astype(BF16), NT)

    row = iota((32, 128), 0)
    lane = iota((32, 128), 1)
    has_next_x = jnp.where(gx < size_x - 1, 1.0, 0.0)
    has_prev_x = jnp.where(gx > 0, 1.0, 0.0)
    has_next_y = jnp.where(gy < size_y - 1, 1.0, 0.0)
    has_prev_y = jnp.where(gy > 0, 1.0, 0.0)
    has_next_z = jnp.where(core == 0, 1.0, 0.0)
    has_prev_z = jnp.where(core == 1, 1.0, 0.0)
    field[...] = jnp.zeros_like(field)
    for x in range(8):
        here = pressure[x]
        after = pressure[x + 1] if x < 7 else from_next_x[pl.ds(192, 32), :] * has_next_x
        before = pressure[x - 1] if x > 0 else from_prev_x[pl.ds(192, 32), :] * has_prev_x
        t_before = trans_x[x - 1] if x > 0 else from_prev_x[pl.ds(224, 32), :] * has_prev_x
        flux = trans_x[x] * (here - after) + t_before * (here - before)
        after = jnp.where(row == 31, from_next_y[pl.ds(48 + x, 1), :] * has_next_y, pltpu.roll(here, 31, 0))
        before = jnp.where(row == 0, from_prev_y[pl.ds(48 + x, 1), :] * has_prev_y, pltpu.roll(here, 1, 0))
        t_here = trans_y[x]
        t_before = jnp.where(row == 0, from_prev_y[pl.ds(56 + x, 1), :] * has_prev_y, pltpu.roll(t_here, 1, 0))
        flux = flux + t_here * (here - after) + t_before * (here - before)
        other = facing_p[x]
        after = jnp.where(lane == 127, pltpu.roll(other, 127, 1) * has_next_z, pltpu.roll(here, 127, 1))
        before = jnp.where(lane == 0, pltpu.roll(other, 1, 1) * has_prev_z, pltpu.roll(here, 1, 1))
        t_here = trans_z[x]
        t_before = jnp.where(lane == 0, pltpu.roll(facing_t[x], 1, 1) * has_prev_z, pltpu.roll(t_here, 1, 1))
        flux = flux + t_here * (here - after) + t_before * (here - before)
        value = source[x] + wells[32 * x : 32 * x + 32] - accumulation[x] * here - flux
        residual[x] = value
        field[pl.ds(40 * x + 2, 32), :] = value

    sums_o[...] = jnp.zeros_like(sums_o)
    sums_z[...] = jnp.zeros_like(sums_z)
    columns = (
        [(from_prev_x, 0, 96, 8, il * 4, il) for il in range(2)],
        [(None, 0, 0, 48, (x + 2) * 4, x) for x in range(8)],
        [(from_next_x, 0, 96, 8, il * 4, 6 + il) for il in range(2)],
    )
    for column, entries in enumerate(columns):
        for by in range(4):
            totals = [None, None]
            for ref, base_o, base_z, step, start, x in entries:
                upper = field[pl.ds(40 * x + 8 * by, 8), :]
                lower = field[pl.ds(40 * x + 8 * by + 8, 4), :]
                for half in range(2):
                    w = ref if ref is not None else (wo, wz)[half]
                    first = (base_o, base_z)[half] + start + by
                    w8 = w[pl.ds(first, 8, stride=step), :]
                    w4 = w[pl.ds(first + 8 * step, 4, stride=step), :]
                    terms = (w8 * upper, w4 * lower)
                    if totals[half] is None:
                        totals[half] = terms
                    else:
                        totals[half] = tuple(a + b for a, b in zip(totals[half], terms))
            for half, sums in enumerate((sums_o, sums_z)):
                a8, a4 = totals[half]
                line = jnp.sum(a8, axis=0, keepdims=True) + jnp.sum(a4, axis=0, keepdims=True)
                sums[pl.ds((by + 1) * 8 + column, 1), :] = line
    for side, (by, ref, first_row) in enumerate(((-1, from_prev_y, 2), (4, from_next_y, 32))):
        for half, sums in enumerate((sums_o, sums_z)):
            lines = [None, None, None]
            for n in range(2):
                strip = field[pl.ds(first_row + n, 8, stride=40), :]
                spot = 2 * n + half
                terms = (
                    (corner_prev[pl.ds(side * 8 + spot * 2, 2), :] * strip[0:2]),
                    (ref[pl.ds(spot * 12 + 2, 8), :] * strip),
                    (corner_next[pl.ds(side * 8 + spot * 2, 2), :] * strip[6:8]),
                )
                for column in range(3):
                    line = jnp.sum(terms[column], axis=0, keepdims=True)
                    lines[column] = line if lines[column] is None else lines[column] + line
            for column in range(3):
                sums[pl.ds((by + 1) * 8 + column, 1), :] = lines[column]
    inside, reach = spread(core)
    out = dot3(sums_o[...], inside) + dot3(sums_z[...], reach)
    level = [out[8 * n : 8 * n + 8] for n in range(6)]
    group = iota((8, 128), 1) // 32
    for zc in range(2):
        total = jnp.zeros((8, 128), F32)
        for by in range(4):
            shift = (by * 32 - zc * 32) % 128
            moved = pltpu.roll(level[by + 1], shift, 1) if shift else level[by + 1]
            total = jnp.where(group == by, moved, total)
        box[pl.ds(8 * zc, 8), :] = total
    box[pl.ds(16, 8), :] = jnp.where(group < 2, level[5], pltpu.roll(level[0], 64, 1))
    box[pl.ds(24, 8), :] = jnp.zeros((8, 128), F32)
    box[pl.ds(24, 1), :] = from_prev_y[pl.ds(64 + 26, 1), :]
    box[pl.ds(25, 1), :] = coarse[pl.ds(26, 1), :]
    box[pl.ds(26, 1), :] = from_next_y[pl.ds(56 + 26, 1), :]


def split_kernel(box, other, own, to_prev, to_next, scale):
    core = lax.axis_index("gz")
    for kind in range(3):
        total = box[pl.ds(8 * kind, 8), :] + other[pl.ds(8 * kind, 8), :]
        to_prev[pl.ds(kind, 1), :] = total[0:1]
        own[pl.ds(kind, 1), :] = total[1:2]
        to_next[pl.ds(kind, 1), :] = total[2:3]
    first = core == 0
    mine = box[pl.ds(24, 8), :]
    theirs = other[pl.ds(24, 8), :]
    low = jnp.where(first, mine, theirs)
    high = jnp.where(first, theirs, mine)
    scale[pl.ds(0, 1), :] = low[1:2]
    scale[pl.ds(1, 1), :] = high[1:2]
    group = iota((1, 128), 1) // 32
    tail = jnp.where(group == 2, pltpu.roll(low[0:1], 96, 1), high[0:1])
    head = jnp.where(group == 0, low[2:3], pltpu.roll(high[2:3], 32, 1))
    scale[pl.ds(2, 1), :] = jnp.where(group < 2, head, tail)


def share_kernel(own, from_prev, from_next, scale, message):
    gx = lax.axis_index("gx")
    size_x = lax.axis_size("gx")
    has_next = jnp.where(gx < size_x - 1, 1.0, 0.0)
    has_prev = jnp.where(gx > 0, 1.0, 0.0)
    total = own[...] + from_prev[...] * has_prev + from_next[...] * has_next
    total = total * scale[...]
    message[...] = jnp.broadcast_to(total[None], message.shape)


OFFSETS = tuple(
    (a, b, c) for a in (-1, 0, 1) for b in (-1, 0, 1) for c in (-1, 0, 1) if (a, b, c) != (0, 0, 0)
)


def solve_kernel(
    shared, near, far, wo, wz, from_prev_x, from_next_x, from_prev_y, from_next_y, corner_prev, corner_next, pressure,
    solution, new_pressure, padded, coefs, start, state, blocks, field,
):
    gx = lax.axis_index("gx")
    gy = lax.axis_index("gy")
    core = lax.axis_index("gz")
    size_x = lax.axis_size("gx")
    size_y = lax.axis_size("gy")

    padded[...] = jnp.zeros_like(padded)
    for x in range(16):
        for y in range(8):
            padded[pl.ds(((x + 4) * 12 + y + 2) * 4, 3), :] = shared[x * 8 + y]
    coefs[pl.ds(pl.multiple_of(core * 672, 8), 672), :] = near[...]
    coefs[pl.ds(pl.multiple_of((1 - core) * 672, 8), 672), :] = far[...]

    lane9 = iota((9, 128), 1)

    def line(dy, kind):
        return padded[pl.ds((gx * 12 + gy + 2 + dy) * 4 + kind, 9, stride=48), :]

    hooks = [line(dy, 2) for dy in range(-2, 3)]
    for yc in range(3):
        valid = jnp.where((gy + yc - 1 >= 0) & (gy + yc - 1 < size_y), 1.0, 0.0)
        below, above = hooks[yc], hooks[yc + 2]
        for zc in range(2):
            first = below if zc == 0 else pltpu.roll(below, 96, 1)
            last = pltpu.roll(above, 32, 1) if zc == 0 else above
            extra = jnp.where(lane9 < 32, first, jnp.where(lane9 >= 96, last, 0.0))
            value = (line(yc - 1, zc) + extra) * valid
            spot = (yc * 2 + zc) * 16
            start[pl.ds(spot, 9), :] = value
            state[pl.ds(spot, 9), :] = value

    lane = iota((7, 128), 1)
    deep = lane % 32
    at_x = iota((7, 128), 0) + gx - 3
    valid_x = (at_x >= 0) & (at_x < size_x)
    for sweep in range(3):
        totals = {}
        for yc in range(3):
            for zc in range(2):
                spot = (yc * 2 + zc) * 16 + 1
                totals[yc, zc] = (1.0 - damping) * state[pl.ds(spot, 7), :] + start[pl.ds(spot, 7), :]
        for a in (-1, 0, 1):
            shifted = {}
            for yc in range(3):
                low = state[pl.ds((yc * 2) * 16 + 1 + a, 7), :]
                high = state[pl.ds((yc * 2 + 1) * 16 + 1 + a, 7), :]
                shifted[yc, 0, 0] = low
                shifted[yc, 1, 0] = high
                shifted[yc, 0, 1] = jnp.where(deep == 31, pltpu.roll(high, 31, 1), pltpu.roll(low, 127, 1))
                shifted[yc, 1, 1] = jnp.where(deep == 31, 0.0, pltpu.roll(high, 127, 1))
                shifted[yc, 0, -1] = jnp.where(deep == 0, 0.0, pltpu.roll(low, 1, 1))
                shifted[yc, 1, -1] = jnp.where(deep == 0, pltpu.roll(low, 97, 1), pltpu.roll(high, 1, 1))
            for c in (-1, 0, 1):
                for zc in range(2):
                    up = [pltpu.roll(shifted[yc, zc, c], 96, 1) for yc in range(3)]
                    down = [pltpu.roll(shifted[yc, zc, c], 32, 1) for yc in range(3)]
                    zero = jnp.zeros((7, 128), F32)
                    for yc in range(3):
                        beyond = up[yc + 1] if yc < 2 else zero
                        behind = down[yc - 1] if yc > 0 else zero
                        values = {
                            -1: jnp.where(lane < 32, behind, down[yc]),
                            0: shifted[yc, zc, c],
                            1: jnp.where(lane >= 96, beyond, up[yc]),
                        }
                        for b in (-1, 0, 1):
                            if (a, b, c) == (0, 0, 0):
                                continue
                            number = OFFSETS.index((a, b, c))
                            coef = coefs[pl.ds(zc * 672 + yc * 32 + number, 7, stride=96), :]
                            totals[yc, zc] = totals[yc, zc] - coef * values[b]
        for yc in range(3):
            valid = valid_x & (gy + yc - 1 >= 0) & (gy + yc - 1 < size_y)
            for zc in range(2):
                state[pl.ds((yc * 2 + zc) * 16 + 1, 7), :] = jnp.where(valid, totals[yc, zc], 0.0)

    low = state[pl.ds(2 * 16 + 4, 1), :]
    high = state[pl.ds(3 * 16 + 4, 1), :]
    mine = jnp.where(core == 0, low, high)
    for by in range(4):
        moved = pltpu.roll(mine, (128 - 32 * by) % 128, 1) if by else mine
        solution[0, pl.ds(by, 1), :] = moved[:, 0:32]

    lane3 = iota((3, 128), 1)
    blocks[...] = jnp.zeros_like(blocks)
    for by in range(-1, 5):
        yc, at = (0, 3) if by < 0 else ((2, 0) if by > 3 else (1, by))
        low = state[pl.ds((yc * 2) * 16 + 3, 3), :]
        high = state[pl.ds((yc * 2 + 1) * 16 + 3, 3), :]
        low = pltpu.roll(low, (128 - 32 * at) % 128, 1) if at else low
        shift = (32 - 32 * at) % 128
        high = pltpu.roll(high, shift, 1) if shift else high
        blocks[pl.ds((by + 1) * 8, 3), :] = jnp.where(lane3 < 32, low, jnp.where(lane3 < 64, high, 0.0))
    inside, reach = spread(core)
    over_o = dot3(blocks[...], inside, NT)
    over_z = dot3(blocks[...], reach, NT)

    def factor(by, column):
        spot = (by + 1) * 8 + column
        return over_o[spot : spot + 1], over_z[spot : spot + 1]

    field[...] = jnp.zeros_like(field)
    for x in range(8):
        entries = [(None, 0, 0, 48, (x + 2) * 4, 1)]
        if x < 2:
            entries.append((from_prev_x, 0, 96, 8, x * 4, 0))
        if x >= 6:
            entries.append((from_next_x, 0, 96, 8, (x - 6) * 4, 2))
        carry = None
        for by in range(4):
            total8 = total4 = None
            for ref, base_o, base_z, step, begin, column in entries:
                factors = factor(by, column)
                for half in range(2):
                    w = ref if ref is not None else (wo, wz)[half]
                    first = (base_o, base_z)[half] + begin + by
                    term8 = w[pl.ds(first, 8, stride=step), :] * factors[half]
                    term4 = w[pl.ds(first + 8 * step, 4, stride=step), :] * factors[half]
                    total8 = term8 if total8 is None else total8 + term8
                    total4 = term4 if total4 is None else total4 + term4
            field[pl.ds(40 * x + 8 * by, 8), :] = total8
            if carry is not None:
                field[pl.ds(40 * x + 8 * by, 4), :] = total8[0:4] + carry
            carry = total4
        field[pl.ds(40 * x + 32, 4), :] = carry
    for side, (by, ref, first_row) in enumerate(((-1, from_prev_y, 2), (4, from_next_y, 32))):
        for n in range(2):
            for half in range(2):
                spot = 2 * n + half
                middle = ref[pl.ds(spot * 12 + 2, 8), :] * factor(by, 1)[half]
                field[pl.ds(first_row + n, 8, stride=40), :] = (
                    field[pl.ds(first_row + n, 8, stride=40), :] + middle
                )
                left = corner_prev[pl.ds(side * 8 + spot * 2, 2), :] * factor(by, 0)[half]
                right = corner_next[pl.ds(side * 8 + spot * 2, 2), :] * factor(by, 2)[half]
                for il in range(2):
                    at = pl.ds(40 * il + first_row + n, 1)
                    field[at, :] = field[at, :] + left[il : il + 1]
                    at = pl.ds(40 * (6 + il) + first_row + n, 1)
                    field[at, :] = field[at, :] + right[il : il + 1]
    for x in range(8):
        new_pressure[x] = pressure[x] + field[pl.ds(40 * x + 2, 32), :]


def call(kernel, out_shapes, scratch=(), name=None):
    single = not isinstance(out_shapes, (list, tuple))
    shapes = [out_shapes] if single else list(out_shapes)
    run = pl.pallas_call(
        kernel,
        out_shape=tuple(shapes) if not single else shapes[0],
        scratch_shapes=list(scratch),
        compiler_params=pltpu.CompilerParams(vmem_limit_bytes=24 * 1024 * 1024),
        name=name,
    )
    return run


def shape(*dims, dtype=F32):
    return jax.ShapeDtypeStruct(dims, dtype)


def shift(value, axis, steps):
    count = lax.axis_size(axis)
    return lax.ppermute(value, axis, [(i, (i + steps) % count) for i in range(count)])


def on_device(
    pressure, accumulation, trans_x, trans_y, trans_z, source, well_cells, well_rates, basis, coarse_off, coarse_diag
):
    core = lax.axis_index("gz")
    tiles = basis.reshape(6, 576, 32)
    plane = lax.dynamic_index_in_dim(tiles, 5 - 5 * core, 0, keepdims=False)
    facing = shift(plane, "gz", 1)
    facing_p = shift(pressure, "gz", 1)
    facing_t = shift(trans_z, "gz", 1)

    inverse = damping / coarse_diag
    coarse = jnp.concatenate([coarse_off * inverse[None], inverse[None]], axis=0).reshape(27, 128)
    coarse = jnp.pad(coarse, ((0, 5), (0, 0)))

    wo, wz, to_next_x, to_prev_x, to_next_y, to_prev_y = call(
        pack_kernel,
        [shape(576, 128), shape(576, 128), shape(256, 128), shape(224, 128), shape(96, 128), shape(88, 128)],
        name="pack",
    )(tiles, facing, pressure, trans_x, trans_y, coarse)
    from_prev_y = shift(to_next_y, "gy", 1)
    from_next_y = shift(to_prev_y, "gy", -1)
    from_prev_x = shift(to_next_x, "gx", 1)
    from_next_x = shift(to_prev_x, "gx", -1)

    strips = jnp.concatenate([from_prev_y[:48], from_next_y[:48]]).reshape(8, 12, 128)
    corner_prev = shift(strips[:, 10:12].reshape(16, 128), "gx", 1)
    corner_next = shift(strips[:, 0:2].reshape(16, 128), "gx", -1)

    column = jnp.concatenate([from_prev_y[64:96], coarse, from_next_y[56:88]])
    near = jnp.concatenate([shift(column, "gx", -d) if d else column for d in range(-3, 4)])
    far = shift(near, "gz", 1)

    residual, box = call(
        restrict_kernel,
        [shape(8, 32, 128), shape(32, 128)],
        [pltpu.VMEM((320, 128), F32), pltpu.VMEM((48, 128), F32), pltpu.VMEM((48, 128), F32)],
        name="restrict",
    )(
        pressure, accumulation, trans_x, trans_y, trans_z, source,
        well_cells.reshape(8, 128), well_rates.reshape(8, 128), facing_p, facing_t, wo, wz,
        from_prev_x, from_next_x, from_prev_y, from_next_y, corner_prev, corner_next, coarse,
    )
    other = shift(box, "gz", 1)
    own, to_prev, to_next, scale = call(split_kernel, [shape(3, 128)] * 4, name="split")(box, other)
    from_next = shift(to_prev, "gx", -1)
    from_prev = shift(to_next, "gx", 1)
    count = lax.axis_size("gx") * lax.axis_size("gy")
    message = call(share_kernel, shape(count, 3, 128), name="share")(own, from_prev, from_next, scale)
    shared = lax.all_to_all(message, ("gx", "gy"), 0, 0)

    solution, new_pressure = call(
        solve_kernel,
        [shape(1, 4, 32), shape(8, 32, 128)],
        [
            pltpu.VMEM((24 * 12 * 4, 128), F32),
            pltpu.VMEM((1344, 128), F32),
            pltpu.VMEM((96, 128), F32),
            pltpu.VMEM((96, 128), F32),
            pltpu.VMEM((48, 128), F32),
            pltpu.VMEM((320, 128), F32),
        ],
        name="solve",
    )(
        shared, near, far, wo, wz, from_prev_x, from_next_x, from_prev_y, from_next_y, corner_prev, corner_next, pressure
    )
    return residual, solution, new_pressure


def solution(mesh):
    cells = P("gx", "gy", "gz")
    in_specs = (
        cells, cells, cells, cells, cells, cells, P(), P(),
        P(None, None, None, "gx", "gy", "gz"), P(None, "gx", "gy", "gz"), cells,
    )
    return jax.shard_map(on_device, mesh=mesh, in_specs=in_specs, out_specs=(cells, cells, cells), check_vma=False)
```

```python
import functools

import jax
import jax.numpy as jnp
from jax import lax
from jax.experimental import pallas as pl
from jax.experimental.pallas import tpu as pltpu
from jax.sharding import PartitionSpec as P

damping = 0.8
F32 = jnp.float32
BF16 = jnp.bfloat16


def iota(shape, dim):
    return lax.broadcasted_iota(jnp.int32, shape, dim)


def parts(a):
    high = a.astype(BF16)
    rest = a - high.astype(F32)
    middle = rest.astype(BF16)
    low = (rest - middle.astype(F32)).astype(BF16)
    return high, middle, low


NN = (((1,), (0,)), ((), ()))
NT = (((1,), (1,)), ((), ()))


def dot(a, b, dims=NN):
    return lax.dot_general(a, b, dims, preferred_element_type=F32)


def dot3(a, b, dims=NN):
    high, middle, low = parts(a)
    return dot(high, b, dims) + dot(middle, b, dims) + dot(low, b, dims)


def spread(core):
    lane = iota((128, 128), 0)
    block = iota((128, 128), 1)
    own = core * 32 + lane // 4
    inside = jnp.where(block == own, 1.0, 0.0).astype(BF16)
    below = (lane % 4 == 0) & (block == own - 1)
    above = (lane % 4 == 3) & (block == own + 1)
    reach = jnp.where(below | above, 1.0, 0.0) * jnp.where(block < 64, 1.0, 0.0)
    return inside, reach.astype(BF16)


def pack_kernel(basis, facing, pressure, trans_y, coarse, wo, wz, to_next_y, to_prev_y):
    core = lax.axis_index("gz")
    block = iota((32, 128), 0)
    lane = iota((32, 128), 1)

    def place(mask):
        return jnp.where(mask, 1.0, 0.0).astype(BF16)

    total = dot(basis[1], place(lane == 4 * block))
    for k in (2, 3, 4):
        total = total + dot(basis[k], place(lane == 4 * block + (k - 1)))
    wo[...] = total
    edge = ((block == 31) & (lane == 0) & (core == 1)) | ((block == 0) & (lane == 127) & (core == 0))
    wz[...] = (
        dot(basis[5], place(lane == 4 * block + 4))
        + dot(basis[0], place(lane == 4 * block - 1))
        + dot(facing[...], place(edge))
    )
    for n in range(2):
        for half, w in enumerate((wo, wz)):
            spot = (2 * n + half) * 12
            to_next_y[pl.ds(spot, 12), :] = w[pl.ds((10 + n) * 48 + 3, 12, stride=4), :]
            to_prev_y[pl.ds(spot, 12), :] = w[pl.ds(n * 48, 12, stride=4), :]
    for x in range(8):
        to_next_y[pl.ds(48 + x, 1), :] = pressure[x, pl.ds(31, 1), :]
        to_next_y[pl.ds(56 + x, 1), :] = trans_y[x, pl.ds(31, 1), :]
        to_prev_y[pl.ds(48 + x, 1), :] = pressure[x, pl.ds(0, 1), :]
    to_next_y[pl.ds(64, 32), :] = coarse[...]
    to_prev_y[pl.ds(56, 32), :] = coarse[...]


def relay_kernel(wo, wz, pressure, trans_x, coarse, from_prev_y, from_next_y, to_next_x, to_prev_x):
    for j in range(12):
        for half, w in enumerate((wo, wz)):
            to_next_x[pl.ds(96 * half + 8 * j, 8), :] = w[pl.ds(48 * j + 40, 8), :]
            to_prev_x[pl.ds(96 * half + 8 * j, 8), :] = w[pl.ds(48 * j, 8), :]
    to_next_x[pl.ds(192, 32), :] = pressure[7]
    to_prev_x[pl.ds(192, 32), :] = pressure[0]
    for side, strip in enumerate((from_prev_y, from_next_y)):
        for spot in range(4):
            to_next_x[pl.ds(224 + side * 8 + spot * 2, 2), :] = strip[pl.ds(spot * 12 + 10, 2), :]
            to_prev_x[pl.ds(224 + side * 8 + spot * 2, 2), :] = strip[pl.ds(spot * 12, 2), :]
    for ref in (to_next_x, to_prev_x):
        ref[pl.ds(240, 32), :] = from_prev_y[pl.ds(64, 32), :]
        ref[pl.ds(272, 32), :] = coarse[...]
        ref[pl.ds(304, 32), :] = from_next_y[pl.ds(56, 32), :]
    to_next_x[pl.ds(336, 32), :] = trans_x[7]


def restrict_kernel(
    pressure, accumulation, trans_x, trans_y, trans_z, source, cells, rates, facing_p, facing_t, wo, wz,
    from_prev_x, from_next_x, from_prev_y, from_next_y,
    residual, mine, theirs, field, sums_o, sums_z,
):
    gx = lax.axis_index("gx")
    gy = lax.axis_index("gy")
    core = lax.axis_index("gz")
    size_x = lax.axis_size("gx")
    size_y = lax.axis_size("gy")

    rows_at = iota((256, 128), 0)
    lane_at = iota((128, 128), 0)
    wells = jnp.zeros((256, 128), F32)
    for c in range(8):
        cell = cells[pl.ds(c, 1), :]
        at_x = (cell >> 16) - gx * 8
        at_y = ((cell >> 8) & 255) - gy * 32
        at_z = (cell & 255) - core * 128
        inside = (at_x >= 0) & (at_x < 8) & (at_y >= 0) & (at_y < 32)
        row = jnp.where(inside, at_x * 32 + at_y, -1)
        hit = jnp.where(row == rows_at, 1.0, 0.0).astype(BF16)
        rate = rates[pl.ds(c, 1), :]
        high, middle, low = parts(rate)
        here = at_z == lane_at
        for part in (high, middle, low):
            wells = wells + dot(hit, jnp.where(here, part.astype(F32), 0.0).astype(BF16), NT)

    row = iota((32, 128), 0)
    lane = iota((32, 128), 1)
    has_next_x = jnp.where(gx < size_x - 1, 1.0, 0.0)
    has_prev_x = jnp.where(gx > 0, 1.0, 0.0)
    has_next_y = jnp.where(gy < size_y - 1, 1.0, 0.0)
    has_prev_y = jnp.where(gy > 0, 1.0, 0.0)
    has_next_z = jnp.where(core == 0, 1.0, 0.0)
    has_prev_z = jnp.where(core == 1, 1.0, 0.0)
    field[...] = jnp.zeros_like(field)
    for x in range(8):
        here = pressure[x]
        after = pressure[x + 1] if x < 7 else from_next_x[pl.ds(192, 32), :] * has_next_x
        before = pressure[x - 1] if x > 0 else from_prev_x[pl.ds(192, 32), :] * has_prev_x
        t_before = trans_x[x - 1] if x > 0 else from_prev_x[pl.ds(336, 32), :] * has_prev_x
        flux = trans_x[x] * (here - after) + t_before * (here - before)
        after = jnp.where(row == 31, from_next_y[pl.ds(48 + x, 1), :] * has_next_y, pltpu.roll(here, 31, 0))
        before = jnp.where(row == 0, from_prev_y[pl.ds(48 + x, 1), :] * has_prev_y, pltpu.roll(here, 1, 0))
        t_here = trans_y[x]
        t_before = jnp.where(row == 0, from_prev_y[pl.ds(56 + x, 1), :] * has_prev_y, pltpu.roll(t_here, 1, 0))
        flux = flux + t_here * (here - after) + t_before * (here - before)
        other = facing_p[x]
        after = jnp.where(lane == 127, pltpu.roll(other, 127, 1) * has_next_z, pltpu.roll(here, 127, 1))
        before = jnp.where(lane == 0, pltpu.roll(other, 1, 1) * has_prev_z, pltpu.roll(here, 1, 1))
        t_here = trans_z[x]
        t_before = jnp.where(lane == 0, pltpu.roll(facing_t[x], 1, 1) * has_prev_z, pltpu.roll(t_here, 1, 1))
        flux = flux + t_here * (here - after) + t_before * (here - before)
        value = source[x] + wells[32 * x : 32 * x + 32] - accumulation[x] * here - flux
        residual[x] = value
        field[pl.ds(40 * x + 2, 32), :] = value

    sums_o[...] = jnp.zeros_like(sums_o)
    sums_z[...] = jnp.zeros_like(sums_z)
    columns = (
        [(from_prev_x, 0, 96, 8, il * 4, il) for il in range(2)],
        [(None, 0, 0, 48, (x + 2) * 4, x) for x in range(8)],
        [(from_next_x, 0, 96, 8, il * 4, 6 + il) for il in range(2)],
    )
    for column, entries in enumerate(columns):
        for by in range(4):
            totals = [None, None]
            for ref, base_o, base_z, step, start, x in entries:
                upper = field[pl.ds(40 * x + 8 * by, 8), :]
                lower = field[pl.ds(40 * x + 8 * by + 8, 4), :]
                for half in range(2):
                    w = ref if ref is not None else (wo, wz)[half]
                    first = (base_o, base_z)[half] + start + by
                    w8 = w[pl.ds(first, 8, stride=step), :]
                    w4 = w[pl.ds(first + 8 * step, 4, stride=step), :]
                    terms = (w8 * upper, w4 * lower)
                    if totals[half] is None:
                        totals[half] = terms
                    else:
                        totals[half] = tuple(a + b for a, b in zip(totals[half], terms))
            for half, sums in enumerate((sums_o, sums_z)):
                a8, a4 = totals[half]
                line = jnp.sum(a8, axis=0, keepdims=True) + jnp.sum(a4, axis=0, keepdims=True)
                sums[pl.ds((by + 1) * 8 + column, 1), :] = line
    for side, (by, ref, first_row) in enumerate(((-1, from_prev_y, 2), (4, from_next_y, 32))):
        for half, sums in enumerate((sums_o, sums_z)):
            lines = [None, None, None]
            for n in range(2):
                strip = field[pl.ds(first_row + n, 8, stride=40), :]
                spot = 2 * n + half
                terms = (
                    (from_prev_x[pl.ds(224 + side * 8 + spot * 2, 2), :] * strip[0:2]),
                    (ref[pl.ds(spot * 12 + 2, 8), :] * strip),
                    (from_next_x[pl.ds(224 + side * 8 + spot * 2, 2), :] * strip[6:8]),
                )
                for column in range(3):
                    line = jnp.sum(terms[column], axis=0, keepdims=True)
                    lines[column] = line if lines[column] is None else lines[column] + line
            for column in range(3):
                sums[pl.ds((by + 1) * 8 + column, 1), :] = lines[column]
    inside, reach = spread(core)
    out = dot3(sums_o[...], inside) + dot3(sums_z[...], reach)
    level = [out[8 * n : 8 * n + 8] for n in range(6)]
    group = iota((8, 128), 1) // 32
    group1 = iota((1, 128), 1) // 32
    halves = []
    for zc in range(2):
        total = jnp.zeros((8, 128), F32)
        for by in range(4):
            shift = (by * 32 - zc * 32) % 128
            moved = pltpu.roll(level[by + 1], shift, 1) if shift else level[by + 1]
            total = jnp.where(group == by, moved, total)
        hooks = [[], []]
        for n in range(4):
            shift = (n * 32 - zc * 32) % 128
            value = level[5] if n % 2 == 0 else level[0]
            value = pltpu.roll(value, shift, 1) if shift else value
            hooks[0].append(value[n // 2 : n // 2 + 1])
            hooks[1].append(value[2:3])
        fourth = jnp.where(
            group1 == 0, hooks[0][0], jnp.where(group1 == 1, hooks[0][1], jnp.where(group1 == 2, hooks[0][2], hooks[0][3]))
        )
        fifth = jnp.where(group1 == 0, hooks[1][0], jnp.where(group1 == 1, hooks[1][1], 0.0))
        halves.append((total[0:3], fourth, fifth))
    first = core == 0
    for target, a, b in ((mine, 0, 1), (theirs, 1, 0)):
        target[pl.ds(0, 3), :] = jnp.where(first, halves[a][0], halves[b][0])
        target[pl.ds(3, 1), :] = jnp.where(first, halves[a][1], halves[b][1])
        target[pl.ds(4, 1), :] = jnp.where(first, halves[a][2], halves[b][2])


def share_kernel(mine, theirs, message, pattern):
    total = mine[...] + theirs[...]
    for n in range(8):
        pattern[pl.ds(5 * n, 5), :] = total
    block = pattern[...]
    for n in range(message.shape[0] // 40):
        message[pl.ds(40 * n, 40), :] = block


def gather_kernel(shared, near, start, padded):
    gx = lax.axis_index("gx")
    gy = lax.axis_index("gy")
    size_x = lax.axis_size("gx")
    size_y = lax.axis_size("gy")
    padded[...] = jnp.zeros_like(padded)
    for x in range(size_x):
        padded[pl.ds((x + 5) * 60 + 10, 40), :] = shared[pl.ds(x * 40, 40), :]
    lane = iota((9, 128), 1)
    at_x = iota((9, 128), 0) + gx - 4
    valid_x = (at_x >= 0) & (at_x < size_x)

    def line(dx, dy, kind):
        return padded[pl.ds(((gx + 1 + dx) * 12 + gy + 2 + dy) * 5 + kind, 9, stride=60), :]

    beyond, before = [], []
    for dy in range(-2, 3):
        a, b, c = line(1, dy, 3), line(0, dy, 3), line(-1, dy, 4)
        beyond.append(a + pltpu.roll(b, 64, 1) + c)
        before.append(pltpu.roll(a, 64, 1) + b + pltpu.roll(c, 64, 1))
    for yc in range(3):
        total = line(1, yc - 1, 0) + line(0, yc - 1, 1) + line(-1, yc - 1, 2)
        total = total + jnp.where(lane < 32, beyond[yc], jnp.where(lane >= 96, before[yc + 2], 0.0))
        total = total * near[pl.ds(yc * 32 + 26, 9, stride=96), :]
        valid = valid_x & (gy + yc - 1 >= 0) & (gy + yc - 1 < size_y)
        start[pl.ds(16 * yc, 9), :] = jnp.where(valid, total, 0.0)


OFFSETS = tuple(
    (a, b, c) for a in (-1, 0, 1) for b in (-1, 0, 1) for c in (-1, 0, 1) if (a, b, c) != (0, 0, 0)
)


def solve_kernel(
    own, other, near, far, wo, wz, from_prev_x, from_next_x, from_prev_y, from_next_y, pressure,
    solution, new_pressure, coefs, start, state, blocks, field,
):
    gx = lax.axis_index("gx")
    gy = lax.axis_index("gy")
    core = lax.axis_index("gz")
    size_x = lax.axis_size("gx")
    size_y = lax.axis_size("gy")

    coefs[pl.ds(pl.multiple_of(core * 864, 8), 864), :] = near[...]
    coefs[pl.ds(pl.multiple_of((1 - core) * 864, 8), 864), :] = far[...]
    for yc in range(3):
        rows = pl.ds(16 * yc, 9)
        mine, theirs = own[rows, :], other[rows, :]
        for zc in range(2):
            value = jnp.where(core == zc, mine, theirs)
            spot = (yc * 2 + zc) * 16
            start[pl.ds(spot, 9), :] = value
            state[pl.ds(spot, 9), :] = value

    lane = iota((7, 128), 1)
    deep = lane % 32
    at_x = iota((7, 128), 0) + gx - 3
    valid_x = (at_x >= 0) & (at_x < size_x)
    for sweep in range(3):
        totals = {}
        for yc in range(3):
            for zc in range(2):
                spot = (yc * 2 + zc) * 16 + 1
                totals[yc, zc] = (1.0 - damping) * state[pl.ds(spot, 7), :] + start[pl.ds(spot, 7), :]
        for a in (-1, 0, 1):
            shifted = {}
            for yc in range(3):
                low = state[pl.ds((yc * 2) * 16 + 1 + a, 7), :]
                high = state[pl.ds((yc * 2 + 1) * 16 + 1 + a, 7), :]
                shifted[yc, 0, 0] = low
                shifted[yc, 1, 0] = high
                shifted[yc, 0, 1] = jnp.where(deep == 31, pltpu.roll(high, 31, 1), pltpu.roll(low, 127, 1))
                shifted[yc, 1, 1] = jnp.where(deep == 31, 0.0, pltpu.roll(high, 127, 1))
                shifted[yc, 0, -1] = jnp.where(deep == 0, 0.0, pltpu.roll(low, 1, 1))
                shifted[yc, 1, -1] = jnp.where(deep == 0, pltpu.roll(low, 97, 1), pltpu.roll(high, 1, 1))
            for c in (-1, 0, 1):
                for zc in range(2):
                    up = [pltpu.roll(shifted[yc, zc, c], 96, 1) for yc in range(3)]
                    down = [pltpu.roll(shifted[yc, zc, c], 32, 1) for yc in range(3)]
                    zero = jnp.zeros((7, 128), F32)
                    for yc in range(3):
                        beyond = up[yc + 1] if yc < 2 else zero
                        behind = down[yc - 1] if yc > 0 else zero
                        values = {
                            -1: jnp.where(lane < 32, behind, down[yc]),
                            0: shifted[yc, zc, c],
                            1: jnp.where(lane >= 96, beyond, up[yc]),
                        }
                        for b in (-1, 0, 1):
                            if (a, b, c) == (0, 0, 0):
                                continue
                            number = OFFSETS.index((a, b, c))
                            coef = coefs[pl.ds(zc * 864 + 96 + yc * 32 + number, 7, stride=96), :]
                            totals[yc, zc] = totals[yc, zc] - coef * values[b]
        for yc in range(3):
            valid = valid_x & (gy + yc - 1 >= 0) & (gy + yc - 1 < size_y)
            for zc in range(2):
                state[pl.ds((yc * 2 + zc) * 16 + 1, 7), :] = jnp.where(valid, totals[yc, zc], 0.0)

    low = state[pl.ds(2 * 16 + 4, 1), :]
    high = state[pl.ds(3 * 16 + 4, 1), :]
    mine = jnp.where(core == 0, low, high)
    for by in range(4):
        moved = pltpu.roll(mine, (128 - 32 * by) % 128, 1) if by else mine
        solution[0, pl.ds(by, 1), :] = moved[:, 0:32]

    lane3 = iota((3, 128), 1)
    blocks[...] = jnp.zeros_like(blocks)
    for by in range(-1, 5):
        yc, at = (0, 3) if by < 0 else ((2, 0) if by > 3 else (1, by))
        low = state[pl.ds((yc * 2) * 16 + 3, 3), :]
        high = state[pl.ds((yc * 2 + 1) * 16 + 3, 3), :]
        low = pltpu.roll(low, (128 - 32 * at) % 128, 1) if at else low
        shift = (32 - 32 * at) % 128
        high = pltpu.roll(high, shift, 1) if shift else high
        blocks[pl.ds((by + 1) * 8, 3), :] = jnp.where(lane3 < 32, low, jnp.where(lane3 < 64, high, 0.0))
    inside, reach = spread(core)
    over_o = dot3(blocks[...], inside, NT)
    over_z = dot3(blocks[...], reach, NT)

    def factor(by, column):
        spot = (by + 1) * 8 + column
        return over_o[spot : spot + 1], over_z[spot : spot + 1]

    field[...] = jnp.zeros_like(field)
    for x in range(8):
        entries = [(None, 0, 0, 48, (x + 2) * 4, 1)]
        if x < 2:
            entries.append((from_prev_x, 0, 96, 8, x * 4, 0))
        if x >= 6:
            entries.append((from_next_x, 0, 96, 8, (x - 6) * 4, 2))
        carry = None
        for by in range(4):
            total8 = total4 = None
            for ref, base_o, base_z, step, begin, column in entries:
                factors = factor(by, column)
                for half in range(2):
                    w = ref if ref is not None else (wo, wz)[half]
                    first = (base_o, base_z)[half] + begin + by
                    term8 = w[pl.ds(first, 8, stride=step), :] * factors[half]
                    term4 = w[pl.ds(first + 8 * step, 4, stride=step), :] * factors[half]
                    total8 = term8 if total8 is None else total8 + term8
                    total4 = term4 if total4 is None else total4 + term4
            field[pl.ds(40 * x + 8 * by, 8), :] = total8
            if carry is not None:
                field[pl.ds(40 * x + 8 * by, 4), :] = total8[0:4] + carry
            carry = total4
        field[pl.ds(40 * x + 32, 4), :] = carry
    for side, (by, ref, first_row) in enumerate(((-1, from_prev_y, 2), (4, from_next_y, 32))):
        for n in range(2):
            for half in range(2):
                spot = 2 * n + half
                middle = ref[pl.ds(spot * 12 + 2, 8), :] * factor(by, 1)[half]
                field[pl.ds(first_row + n, 8, stride=40), :] = (
                    field[pl.ds(first_row + n, 8, stride=40), :] + middle
                )
                left = from_prev_x[pl.ds(224 + side * 8 + spot * 2, 2), :] * factor(by, 0)[half]
                right = from_next_x[pl.ds(224 + side * 8 + spot * 2, 2), :] * factor(by, 2)[half]
                for il in range(2):
                    at = pl.ds(40 * il + first_row + n, 1)
                    field[at, :] = field[at, :] + left[il : il + 1]
                    at = pl.ds(40 * (6 + il) + first_row + n, 1)
                    field[at, :] = field[at, :] + right[il : il + 1]
    for x in range(8):
        new_pressure[x] = pressure[x] + field[pl.ds(40 * x + 2, 32), :]


def call(kernel, out_shapes, scratch=(), name=None):
    single = not isinstance(out_shapes, (list, tuple))
    shapes = [out_shapes] if single else list(out_shapes)
    run = pl.pallas_call(
        kernel,
        out_shape=tuple(shapes) if not single else shapes[0],
        scratch_shapes=list(scratch),
        compiler_params=pltpu.CompilerParams(vmem_limit_bytes=24 * 1024 * 1024),
        name=name,
    )
    return run


def shape(*dims, dtype=F32):
    return jax.ShapeDtypeStruct(dims, dtype)


def shift(value, axis, steps):
    count = lax.axis_size(axis)
    return lax.ppermute(value, axis, [(i, (i + steps) % count) for i in range(count)])


def on_device(
    pressure, accumulation, trans_x, trans_y, trans_z, source, well_cells, well_rates, basis, coarse_off, coarse_diag
):
    core = lax.axis_index("gz")
    tiles = basis.reshape(6, 576, 32)
    plane = lax.dynamic_index_in_dim(tiles, 5 - 5 * core, 0, keepdims=False)
    facing = shift(plane, "gz", 1)
    facing_p = shift(pressure, "gz", 1)
    facing_t = shift(trans_z, "gz", 1)

    inverse = damping / coarse_diag
    coarse = jnp.concatenate([coarse_off * inverse[None], inverse[None]], axis=0).reshape(27, 128)
    coarse = jnp.pad(coarse, ((0, 5), (0, 0)))

    wo, wz, to_next_y, to_prev_y = call(
        pack_kernel, [shape(576, 128), shape(576, 128), shape(96, 128), shape(88, 128)], name="pack"
    )(tiles, facing, pressure, trans_y, coarse)
    from_prev_y = shift(to_next_y, "gy", 1)
    from_next_y = shift(to_prev_y, "gy", -1)
    to_next_x, to_prev_x = call(relay_kernel, [shape(368, 128), shape(336, 128)], name="relay")(
        wo, wz, pressure, trans_x, coarse, from_prev_y, from_next_y
    )
    from_prev_x = shift(to_next_x, "gx", 1)
    from_next_x = shift(to_prev_x, "gx", -1)

    residual, mine, theirs = call(
        restrict_kernel,
        [shape(8, 32, 128), shape(5, 128), shape(5, 128)],
        [pltpu.VMEM((320, 128), F32), pltpu.VMEM((48, 128), F32), pltpu.VMEM((48, 128), F32)],
        name="restrict",
    )(
        pressure, accumulation, trans_x, trans_y, trans_z, source,
        well_cells.reshape(8, 128), well_rates.reshape(8, 128), facing_p, facing_t, wo, wz,
        from_prev_x, from_next_x, from_prev_y, from_next_y,
    )
    count = lax.axis_size("gx") * lax.axis_size("gy")
    message = call(share_kernel, shape(5 * count, 128), [pltpu.VMEM((40, 128), F32)], name="share")(
        mine, shift(theirs, "gz", 1)
    )
    shared = lax.all_to_all(message.reshape(count, 1, 640), ("gx", "gy"), 0, 0).reshape(5 * count, 128)

    column = jnp.concatenate([from_prev_x[240:336], to_next_x[240:336], from_next_x[240:336]])
    near = jnp.concatenate([shift(column, "gx", 3), column, shift(column, "gx", -3)])
    far = shift(near, "gz", 1)

    own = call(gather_kernel, shape(48, 128), [pltpu.VMEM((26 * 60, 128), F32)], name="gather")(shared, near)
    other = shift(own, "gz", 1)
    solution, new_pressure = call(
        solve_kernel,
        [shape(1, 4, 32), shape(8, 32, 128)],
        [
            pltpu.VMEM((1728, 128), F32),
            pltpu.VMEM((96, 128), F32),
            pltpu.VMEM((96, 128), F32),
            pltpu.VMEM((48, 128), F32),
            pltpu.VMEM((320, 128), F32),
        ],
        name="solve",
    )(own, other, near, far, wo, wz, from_prev_x, from_next_x, from_prev_y, from_next_y, pressure)
    return residual, solution, new_pressure


def solution(mesh):
    cells = P("gx", "gy", "gz")
    in_specs = (
        cells, cells, cells, cells, cells, cells, P(), P(),
        P(None, None, None, "gx", "gy", "gz"), P(None, "gx", "gy", "gz"), cells,
    )
    return jax.shard_map(on_device, mesh=mesh, in_specs=in_specs, out_specs=(cells, cells, cells), check_vma=False)
```

```python
import jax
import jax.numpy as jnp
from jax import lax
from jax.experimental import pallas as pl
from jax.experimental.pallas import tpu as pltpu
from jax.sharding import PartitionSpec as P


damping = 0.8
F32 = jnp.float32
BF16 = jnp.bfloat16


def iota(shape, dim):
    return lax.broadcasted_iota(jnp.int32, shape, dim)


def parts(a):
    high = a.astype(BF16)
    rest = a - high.astype(F32)
    middle = rest.astype(BF16)
    low = (rest - middle.astype(F32)).astype(BF16)
    return high, middle, low


NN = (((1,), (0,)), ((), ()))
NT = (((1,), (1,)), ((), ()))


def dot(a, b, dims=NN):
    return lax.dot_general(a, b, dims, preferred_element_type=F32)


def dot3(a, b, dims=NN):
    high, middle, low = parts(a)
    return dot(high, b, dims) + dot(middle, b, dims) + dot(low, b, dims)


def spread(core):
    lane = iota((128, 128), 0)
    block = iota((128, 128), 1)
    block = jnp.where(block < 64, block, 32 - core)
    own = core * 32 + lane // 4
    inside = jnp.where(block == own, 1.0, 0.0).astype(BF16)
    below = (lane % 4 == 0) & (block == own - 1)
    above = (lane % 4 == 3) & (block == own + 1)
    return inside, jnp.where(below | above, 1.0, 0.0).astype(BF16)


def faced(core, mine, theirs):
    lane = iota(mine.shape, 1)
    return mine + jnp.where(lane == 127 - 127 * core, pltpu.roll(theirs, 126 + core, 1), 0.0)


def pack_kernel(
    basis_in, pressure_in, trans_y_in, coarse_off_in, coarse_diag_in, wo, wz, to_next_y, to_prev_y, coarse,
    basis, pressure, trans_y, coarse_off, coarse_diag, done,
):
    copies = [
        pltpu.make_async_copy(source, target, done.at[n])
        for n, (source, target) in enumerate(
            (
                (basis_in, basis),
                (coarse_off_in, coarse_off),
                (coarse_diag_in, coarse_diag),
                (pressure_in, pressure),
                (trans_y_in, trans_y),
            )
        )
    ]
    for copy in copies:
        copy.start()
    core = lax.axis_index("gz")
    block = iota((32, 128), 0)
    lane = iota((32, 128), 1)

    def place(mask):
        return jnp.where(mask, 1.0, 0.0).astype(BF16)

    for copy in copies:
        copy.wait()
    total = dot(basis[1], place(lane == 4 * block))
    for k in (2, 3, 4):
        total = total + dot(basis[k], place(lane == 4 * block + (k - 1)))
    wo[...] = total
    wz[...] = dot(basis[5], place((lane == 4 * block + 4) | ((block == 31) & (lane == 1) & (core == 0)))) + dot(
        basis[0], place((lane == 4 * block - 1) | ((block == 0) & (lane == 1) & (core == 1)))
    )
    for n in range(2):
        for half, w in enumerate((wo, wz)):
            spot = (2 * n + half) * 12
            to_next_y[pl.ds(spot, 12), :] = w[pl.ds((10 + n) * 48 + 3, 12, stride=4), :]
            to_prev_y[pl.ds(spot, 12), :] = w[pl.ds(n * 48, 12, stride=4), :]
    for x in range(8):
        to_next_y[pl.ds(48 + x, 1), :] = pressure[x, pl.ds(31, 1), :]
        to_next_y[pl.ds(56 + x, 1), :] = trans_y[x, pl.ds(31, 1), :]
        to_prev_y[pl.ds(48 + x, 1), :] = pressure[x, pl.ds(0, 1), :]
    inverse = damping / coarse_diag[0]
    total = jnp.zeros((26, 128), F32)
    line = jnp.zeros((1, 128), F32)
    for by in range(4):
        spot = place(lane == 32 * by + block)
        scale = inverse[by : by + 1]
        total = total + dot3(coarse_off[:, 0, by, :] * scale, spot)
        line = line + dot3(jnp.broadcast_to(scale, (8, 32)), spot)[0:1]
    coarse[...] = jnp.zeros_like(coarse)
    coarse[pl.ds(0, 26), :] = total
    coarse[pl.ds(26, 1), :] = line
    to_next_y[pl.ds(64, 32), :] = coarse[...]
    to_prev_y[pl.ds(56, 32), :] = coarse[...]


def relay_kernel(wo, wz, facing, pressure, trans_x, coarse, from_prev_y, from_next_y, whole, to_next_x, to_prev_x, strips):
    core = lax.axis_index("gz")
    whole[...] = faced(core, wz[...], facing[...])
    for j in range(12):
        for half, w in enumerate((wo, whole)):
            to_next_x[pl.ds(96 * half + 8 * j, 8), :] = w[pl.ds(48 * j + 40, 8), :]
            to_prev_x[pl.ds(96 * half + 8 * j, 8), :] = w[pl.ds(48 * j, 8), :]
    to_next_x[pl.ds(192, 32), :] = pressure[7]
    to_prev_x[pl.ds(192, 32), :] = pressure[0]
    for side, strip in enumerate((from_prev_y, from_next_y)):
        for n in range(2):
            strips[pl.ds(side * 24 + n * 12, 12), :] = strip[pl.ds((2 * n + 1) * 12, 12), :]
        for spot in range(4):
            to_next_x[pl.ds(224 + side * 8 + spot * 2, 2), :] = strip[pl.ds(spot * 12 + 10, 2), :]
            to_prev_x[pl.ds(224 + side * 8 + spot * 2, 2), :] = strip[pl.ds(spot * 12, 2), :]
    for ref in (to_next_x, to_prev_x):
        ref[pl.ds(240, 32), :] = from_prev_y[pl.ds(64, 32), :]
        ref[pl.ds(272, 32), :] = coarse[...]
        ref[pl.ds(304, 32), :] = from_next_y[pl.ds(56, 32), :]
    to_next_x[pl.ds(336, 32), :] = trans_x[7]


def collect_kernel(from_prev_x, from_next_x, own, corners, up, down):
    corners[pl.ds(0, 16), :] = from_prev_x[pl.ds(224, 16), :]
    corners[pl.ds(16, 16), :] = from_next_x[pl.ds(224, 16), :]
    at = iota((96, 128), 0) % 32

    def narrow(rows):
        rest = rows - rows.astype(BF16).astype(F32)
        return jnp.where(at == 27, pltpu.roll(rest, 1, 0), rows).astype(BF16)

    for ref, far, near in ((up, from_prev_x, from_next_x), (down, from_next_x, from_prev_x)):
        outer = narrow(far[pl.ds(240, 96), :]).astype(F32)
        inverses = [outer[32 * yc + 24 : 32 * yc + 32] for yc in range(3)]
        ref[pl.ds(0, 32), :] = jnp.concatenate(inverses + [jnp.zeros((8, 128), F32)], axis=0).astype(BF16)
        ref[pl.ds(32, 96), :] = narrow(own[pl.ds(240, 96), :])
        ref[pl.ds(128, 96), :] = narrow(near[pl.ds(240, 96), :])


def window_kernel(up, down, from_prev_x, own, from_next_x, near):
    def wide(rows):
        rows = rows.astype(F32)
        at = iota(rows.shape, 0) % 32
        return rows + jnp.where(at == 26, pltpu.roll(rows, rows.shape[0] - 1, 0), 0.0)

    for spot, ref in ((0, up), (680, down)):
        near[pl.ds(spot, 8), :] = jnp.zeros((8, 128), F32)
        outer = ref[pl.ds(0, 32), :].astype(F32)
        for yc in range(3):
            near[pl.ds(spot + yc, 1), :] = outer[8 * yc + 2 : 8 * yc + 3] + outer[8 * yc + 3 : 8 * yc + 4]
    near[pl.ds(8, 96), :] = wide(up[pl.ds(32, 96), :])
    near[pl.ds(104, 96), :] = wide(up[pl.ds(128, 96), :])
    near[pl.ds(200, 96), :] = from_prev_x[pl.ds(240, 96), :]
    near[pl.ds(296, 96), :] = own[pl.ds(240, 96), :]
    near[pl.ds(392, 96), :] = from_next_x[pl.ds(240, 96), :]
    near[pl.ds(488, 96), :] = wide(down[pl.ds(128, 96), :])
    near[pl.ds(584, 96), :] = wide(down[pl.ds(32, 96), :])


def stack_kernel(near, far, coefs):
    core = lax.axis_index("gz")
    coefs[pl.ds(pl.multiple_of(core * 688, 8), 688), :] = near[...]
    coefs[pl.ds(pl.multiple_of((1 - core) * 688, 8), 688), :] = far[...]


def wells_kernel(cells, rates, wells):
    gx = lax.axis_index("gx")
    gy = lax.axis_index("gy")
    core = lax.axis_index("gz")
    rows_at = iota((256, 128), 0)
    lane_at = iota((128, 128), 0)
    total = jnp.zeros((256, 128), F32)
    for c in range(8):
        cell = cells[pl.ds(c, 1), :]
        at_x = (cell >> 16) - gx * 8
        at_y = ((cell >> 8) & 255) - gy * 32
        at_z = (cell & 255) - core * 128
        inside = (at_x >= 0) & (at_x < 8) & (at_y >= 0) & (at_y < 32)
        row = jnp.where(inside, at_x * 32 + at_y, -1)
        hit = jnp.where(row == rows_at, 1.0, 0.0).astype(BF16)
        here = at_z == lane_at
        for part in parts(rates[pl.ds(c, 1), :]):
            total = total + dot(hit, jnp.where(here, part.astype(F32), 0.0).astype(BF16), NT)
    wells[...] = total


def local_kernel(
    pressure, accumulation, trans_x, trans_y, trans_z, source, wells, facing_p, facing_t, from_prev_y, from_next_y, partial
):
    gy = lax.axis_index("gy")
    core = lax.axis_index("gz")
    size_y = lax.axis_size("gy")
    row = iota((32, 128), 0)
    lane = iota((32, 128), 1)
    has_next_y = jnp.where(gy < size_y - 1, 1.0, 0.0)
    has_prev_y = jnp.where(gy > 0, 1.0, 0.0)
    has_next_z = jnp.where(core == 0, 1.0, 0.0)
    has_prev_z = jnp.where(core == 1, 1.0, 0.0)
    for x in range(8):
        here = pressure[x]
        flux = jnp.zeros((32, 128), F32)
        if x < 7:
            flux = flux + trans_x[x] * (here - pressure[x + 1])
        if x > 0:
            flux = flux + trans_x[x - 1] * (here - pressure[x - 1])
        after = jnp.where(row == 31, from_next_y[pl.ds(48 + x, 1), :] * has_next_y, pltpu.roll(here, 31, 0))
        before = jnp.where(row == 0, from_prev_y[pl.ds(48 + x, 1), :] * has_prev_y, pltpu.roll(here, 1, 0))
        t_here = trans_y[x]
        t_before = jnp.where(row == 0, from_prev_y[pl.ds(56 + x, 1), :] * has_prev_y, pltpu.roll(t_here, 1, 0))
        flux = flux + t_here * (here - after) + t_before * (here - before)
        other = facing_p[x]
        after = jnp.where(lane == 127, pltpu.roll(other, 127, 1) * has_next_z, pltpu.roll(here, 127, 1))
        before = jnp.where(lane == 0, pltpu.roll(other, 1, 1) * has_prev_z, pltpu.roll(here, 1, 1))
        t_here = trans_z[x]
        t_before = jnp.where(lane == 0, pltpu.roll(facing_t[x], 1, 1) * has_prev_z, pltpu.roll(t_here, 1, 1))
        flux = flux + t_here * (here - after) + t_before * (here - before)
        partial[x] = source[x] + wells[pl.ds(32 * x, 32), :] - accumulation[x] * here - flux


def sums_kernel(
    partial, pressure, trans_x, wo, wz, from_prev_x, from_next_x, from_prev_y, from_next_y, facing_y,
    residual, field, sums_o, sums_z,
):
    gx = lax.axis_index("gx")
    core = lax.axis_index("gz")
    size_x = lax.axis_size("gx")
    has_next_x = jnp.where(gx < size_x - 1, 1.0, 0.0)
    has_prev_x = jnp.where(gx > 0, 1.0, 0.0)
    field[...] = jnp.zeros_like(field)
    for x in range(8):
        value = partial[x]
        here = pressure[x]
        if x == 0:
            value = value - from_prev_x[pl.ds(336, 32), :] * has_prev_x * (
                here - from_prev_x[pl.ds(192, 32), :] * has_prev_x
            )
        if x == 7:
            value = value - trans_x[7] * (here - from_next_x[pl.ds(192, 32), :] * has_next_x)
        residual[x] = value
        field[pl.ds(40 * x + 2, 32), :] = value
    sums_o[...] = jnp.zeros_like(sums_o)
    sums_z[...] = jnp.zeros_like(sums_z)
    columns = (
        [(from_prev_x, 0, 96, 8, il * 4, il) for il in range(2)],
        [(None, 0, 0, 48, (x + 2) * 4, x) for x in range(8)],
        [(from_next_x, 0, 96, 8, il * 4, 6 + il) for il in range(2)],
    )
    for column, entries in enumerate(columns):
        for by in range(4):
            totals = [None, None]
            for ref, base_o, base_z, step, start, x in entries:
                upper = field[pl.ds(40 * x + 8 * by, 8), :]
                lower = field[pl.ds(40 * x + 8 * by + 8, 4), :]
                for half in range(2):
                    w = ref if ref is not None else (wo, wz)[half]
                    first = (base_o, base_z)[half] + start + by
                    w8 = w[pl.ds(first, 8, stride=step), :]
                    w4 = w[pl.ds(first + 8 * step, 4, stride=step), :]
                    terms = (w8 * upper, w4 * lower)
                    if totals[half] is None:
                        totals[half] = terms
                    else:
                        totals[half] = tuple(a + b for a, b in zip(totals[half], terms))
            for half, sums in enumerate((sums_o, sums_z)):
                a8, a4 = totals[half]
                line = jnp.sum(a8, axis=0, keepdims=True) + jnp.sum(a4, axis=0, keepdims=True)
                sums[pl.ds((by + 1) * 8 + column, 1), :] = line
    for side, (by, first_row, strip) in enumerate(((-1, 2, from_prev_y), (4, 32, from_next_y))):
        for half, sums in enumerate((sums_o, sums_z)):
            total = None
            for n in range(2):
                tile = strip[pl.ds((2 * n + half) * 12 + 2, 8), :]
                if half:
                    tile = faced(core, tile, facing_y[pl.ds(side * 24 + n * 12 + 2, 8), :])
                line = tile * field[pl.ds(first_row + n, 8, stride=40), :]
                total = line if total is None else total + line
            sums[pl.ds((by + 1) * 8 + 1, 1), :] = jnp.sum(total, axis=0, keepdims=True)


def tail_kernel(field, sums_o, sums_z, corners, facing_x, message, whole, done_o, done_z, pattern):
    core = lax.axis_index("gz")
    at = iota((32, 128), 0)
    whole[...] = jnp.where((at % 8) // 2 % 2 == 1, faced(core, corners[...], facing_x[...]), corners[...])
    done_o[...] = sums_o[...]
    done_z[...] = sums_z[...]
    for side, (by, first_row) in enumerate(((-1, 2), (4, 32))):
        for half, sums in enumerate((done_o, done_z)):
            for column, first_x in ((0, 0), (2, 6)):
                total = None
                for n in range(2):
                    tile = whole[pl.ds(column * 8 + side * 8 + (2 * n + half) * 2, 2), :]
                    line = tile * field[pl.ds(40 * first_x + first_row + n, 2, stride=40), :]
                    total = line if total is None else total + line
                sums[pl.ds((by + 1) * 8 + column, 1), :] = jnp.sum(total, axis=0, keepdims=True)
    inside, reach = spread(core)
    out = dot3(done_o[...], inside) + dot3(done_z[...], reach)
    level = [out[8 * n : 8 * n + 8] for n in range(6)]
    group = iota((8, 128), 1) // 32
    group1 = iota((1, 128), 1) // 32
    halves = []
    for zc in range(2):
        total = jnp.zeros((8, 128), F32)
        for by in range(4):
            shift = (by * 32 - zc * 32) % 128
            moved = pltpu.roll(level[by + 1], shift, 1) if shift else level[by + 1]
            total = jnp.where(group == by, moved, total)
        hooks = [[], []]
        for n in range(4):
            shift = (n * 32 - zc * 32) % 128
            value = level[5] if n % 2 == 0 else level[0]
            value = pltpu.roll(value, shift, 1) if shift else value
            hooks[0].append(value[n // 2 : n // 2 + 1])
            hooks[1].append(value[2:3])
        fourth = jnp.where(
            group1 == 0, hooks[0][0], jnp.where(group1 == 1, hooks[0][1], jnp.where(group1 == 2, hooks[0][2], hooks[0][3]))
        )
        fifth = jnp.where(group1 == 0, hooks[1][0], hooks[1][1])
        halves.append((total[0:3], fourth, fifth))
    first = core == 0
    row = iota((48, 128), 0)
    mask = (iota((48, 128), 1) == 64 + (row // 8) * 4 + row % 8) & (row % 8 < 3)
    across = jnp.sum(jnp.where(mask, out, 0.0), axis=0, keepdims=True)
    for n in range(8):
        pattern[pl.ds(5 * n, 3), :] = jnp.where(first, halves[0][0], halves[1][0])
        pattern[pl.ds(5 * n + 3, 1), :] = jnp.where(first, halves[0][1], halves[1][1])
        pattern[pl.ds(5 * n + 4, 1), :] = jnp.where(
            group1 < 2, jnp.where(first, halves[0][2], halves[1][2]), across
        )
    block = pattern[...]
    for n in range(message.shape[0] // 40):
        message[pl.ds(40 * n, 40), :] = block


def gather_kernel(shared, own, padded):
    gx = lax.axis_index("gx")
    gy = lax.axis_index("gy")
    core = lax.axis_index("gz")
    size_x = lax.axis_size("gx")
    padded[...] = jnp.zeros_like(padded)
    for x in range(size_x):
        padded[pl.ds((x + 5) * 60 + 10, 40), :] = shared[pl.ds(x * 40, 40), :]
    lane = iota((9, 128), 1)
    source = iota((128, 128), 0)
    target = iota((128, 128), 1)
    edge = 31 * core
    at = target // 32
    hit = target % 32 == edge

    def place(mask):
        return jnp.where(mask, 1.0, 0.0).astype(BF16)

    within = place(hit & (source == 68 + 4 * at))
    lower = place(hit & (at == 0) & (source == 84))
    upper = place(hit & (at == 3) & (source == 64))

    def line(dx, dy, kind):
        return padded[pl.ds(((gx + 1 + dx) * 12 + gy + 2 + dy) * 5 + kind, 9, stride=60), :]

    beyond, before, across = [], [], []
    for dy in range(-2, 3):
        a, b, c, d, e = line(1, dy, 3), line(0, dy, 3), line(-1, dy, 4), line(1, dy, 4), line(0, dy, 4)
        beyond.append(a + pltpu.roll(b, 64, 1) + c)
        before.append(pltpu.roll(a, 64, 1) + b + pltpu.roll(c, 64, 1))
        across.append(d + pltpu.roll(e, 127, 1) + pltpu.roll(c, 126, 1))
    own[...] = jnp.zeros_like(own)
    for yc in range(3):
        total = line(1, yc - 1, 0) + line(0, yc - 1, 1) + line(-1, yc - 1, 2)
        total = total + jnp.where(lane < 32, beyond[yc], jnp.where(lane >= 96, before[yc + 2], 0.0))
        own[pl.ds(16 * yc, 9), :] = total
        own[pl.ds(48 + 16 * yc, 9), :] = (
            dot3(across[yc + 1], within) + dot3(across[yc], lower) + dot3(across[yc + 2], upper)
        )


OFFSETS = tuple(
    (a, b, c) for a in (-1, 0, 1) for b in (-1, 0, 1) for c in (-1, 0, 1) if (a, b, c) != (0, 0, 0)
)


def solve_kernel(
    own, other, coefs, wo, wz, from_prev_x, from_next_x, from_prev_y, from_next_y, facing_y, corners, pressure,
    solution, new_pressure, start, state, blocks, field,
):
    gx = lax.axis_index("gx")
    gy = lax.axis_index("gy")
    core = lax.axis_index("gz")
    size_x = lax.axis_size("gx")
    size_y = lax.axis_size("gy")

    at_x = iota((9, 128), 0) + gx - 4
    valid_x = (at_x >= 0) & (at_x < size_x)
    for yc in range(3):
        mine = own[pl.ds(16 * yc, 9), :] + other[pl.ds(48 + 16 * yc, 9), :]
        theirs = other[pl.ds(16 * yc, 9), :] + own[pl.ds(48 + 16 * yc, 9), :]
        valid = valid_x & (gy + yc - 1 >= 0) & (gy + yc - 1 < size_y)
        for zc in range(2):
            spot = (yc * 2 + zc) * 16
            base = zc * 688
            state[pl.ds(spot, 1), :] = coefs[pl.ds(base + yc, 1), :]
            state[pl.ds(spot + 1, 7), :] = coefs[pl.ds(base + 8 + yc * 32 + 26, 7, stride=96), :]
            state[pl.ds(spot + 8, 1), :] = coefs[pl.ds(base + 680 + yc, 1), :]
            value = jnp.where(core == zc, mine, theirs) * state[pl.ds(spot, 9), :]
            value = jnp.where(valid, value, 0.0)
            start[pl.ds(spot, 9), :] = value
            state[pl.ds(spot, 9), :] = value

    lane = iota((7, 128), 1)
    deep = lane % 32
    at_x = iota((7, 128), 0) + gx - 3
    valid_x = (at_x >= 0) & (at_x < size_x)
    for _ in range(3):
        totals = {}
        for yc in range(3):
            for zc in range(2):
                spot = (yc * 2 + zc) * 16 + 1
                totals[yc, zc] = (1.0 - damping) * state[pl.ds(spot, 7), :] + start[pl.ds(spot, 7), :]
        for a in (-1, 0, 1):
            shifted = {}
            for yc in range(3):
                low = state[pl.ds((yc * 2) * 16 + 1 + a, 7), :]
                high = state[pl.ds((yc * 2 + 1) * 16 + 1 + a, 7), :]
                shifted[yc, 0, 0] = low
                shifted[yc, 1, 0] = high
                shifted[yc, 0, 1] = jnp.where(deep == 31, pltpu.roll(high, 31, 1), pltpu.roll(low, 127, 1))
                shifted[yc, 1, 1] = jnp.where(deep == 31, 0.0, pltpu.roll(high, 127, 1))
                shifted[yc, 0, -1] = jnp.where(deep == 0, 0.0, pltpu.roll(low, 1, 1))
                shifted[yc, 1, -1] = jnp.where(deep == 0, pltpu.roll(low, 97, 1), pltpu.roll(high, 1, 1))
            for c in (-1, 0, 1):
                for zc in range(2):
                    up = [pltpu.roll(shifted[yc, zc, c], 96, 1) for yc in range(3)]
                    down = [pltpu.roll(shifted[yc, zc, c], 32, 1) for yc in range(3)]
                    zero = jnp.zeros((7, 128), F32)
                    for yc in range(3):
                        beyond = up[yc + 1] if yc < 2 else zero
                        behind = down[yc - 1] if yc > 0 else zero
                        values = {
                            -1: jnp.where(lane < 32, behind, down[yc]),
                            0: shifted[yc, zc, c],
                            1: jnp.where(lane >= 96, beyond, up[yc]),
                        }
                        for b in (-1, 0, 1):
                            if (a, b, c) == (0, 0, 0):
                                continue
                            number = OFFSETS.index((a, b, c))
                            coef = coefs[pl.ds(zc * 688 + 8 + yc * 32 + number, 7, stride=96), :]
                            totals[yc, zc] = totals[yc, zc] - coef * values[b]
        for yc in range(3):
            valid = valid_x & (gy + yc - 1 >= 0) & (gy + yc - 1 < size_y)
            for zc in range(2):
                state[pl.ds((yc * 2 + zc) * 16 + 1, 7), :] = jnp.where(valid, totals[yc, zc], 0.0)

    low = state[pl.ds(2 * 16 + 4, 1), :]
    high = state[pl.ds(3 * 16 + 4, 1), :]
    mine = jnp.where(core == 0, low, high)
    for by in range(4):
        moved = pltpu.roll(mine, (128 - 32 * by) % 128, 1) if by else mine
        solution[0, pl.ds(by, 1), :] = moved[:, 0:32]

    lane3 = iota((3, 128), 1)
    blocks[...] = jnp.zeros_like(blocks)
    for by in range(-1, 5):
        yc, at = (0, 3) if by < 0 else ((2, 0) if by > 3 else (1, by))
        low = state[pl.ds((yc * 2) * 16 + 3, 3), :]
        high = state[pl.ds((yc * 2 + 1) * 16 + 3, 3), :]
        low = pltpu.roll(low, (128 - 32 * at) % 128, 1) if at else low
        shift = (32 - 32 * at) % 128
        high = pltpu.roll(high, shift, 1) if shift else high
        blocks[pl.ds((by + 1) * 8, 3), :] = jnp.where(lane3 < 32, low, jnp.where(lane3 < 64, high, 0.0))
    inside, reach = spread(core)
    over_o = dot3(blocks[...], inside, NT)
    over_z = dot3(blocks[...], reach, NT)

    def factor(by, column):
        spot = (by + 1) * 8 + column
        return over_o[spot : spot + 1], over_z[spot : spot + 1]

    field[...] = jnp.zeros_like(field)
    for x in range(8):
        entries = [(None, 0, 0, 48, (x + 2) * 4, 1)]
        if x < 2:
            entries.append((from_prev_x, 0, 96, 8, x * 4, 0))
        if x >= 6:
            entries.append((from_next_x, 0, 96, 8, (x - 6) * 4, 2))
        carry = None
        for by in range(4):
            total8 = total4 = None
            for ref, base_o, base_z, step, begin, column in entries:
                factors = factor(by, column)
                for half in range(2):
                    w = ref if ref is not None else (wo, wz)[half]
                    first = (base_o, base_z)[half] + begin + by
                    term8 = w[pl.ds(first, 8, stride=step), :] * factors[half]
                    term4 = w[pl.ds(first + 8 * step, 4, stride=step), :] * factors[half]
                    total8 = term8 if total8 is None else total8 + term8
                    total4 = term4 if total4 is None else total4 + term4
            field[pl.ds(40 * x + 8 * by, 8), :] = total8
            if carry is not None:
                field[pl.ds(40 * x + 8 * by, 4), :] = total8[0:4] + carry
            carry = total4
        field[pl.ds(40 * x + 32, 4), :] = carry
    for side, (by, first_row, strip) in enumerate(((-1, 2, from_prev_y), (4, 32, from_next_y))):
        for n in range(2):
            middle = strip[pl.ds(2 * n * 12 + 2, 8), :] * factor(by, 1)[0]
            tile = faced(core, strip[pl.ds((2 * n + 1) * 12 + 2, 8), :], facing_y[pl.ds(side * 24 + n * 12 + 2, 8), :])
            middle = middle + tile * factor(by, 1)[1]
            rows = pl.ds(first_row + n, 8, stride=40)
            field[rows, :] = field[rows, :] + middle
            for column, first_x in ((0, 0), (2, 6)):
                spot = column * 8 + side * 8 + n * 4
                factors = factor(by, column)
                rows = pl.ds(40 * first_x + first_row + n, 2, stride=40)
                field[rows, :] = (
                    field[rows, :]
                    + corners[pl.ds(spot, 2), :] * factors[0]
                    + corners[pl.ds(spot + 2, 2), :] * factors[1]
                )
    for x in range(8):
        new_pressure[x] = pressure[x] + field[pl.ds(40 * x + 2, 32), :]


def call(kernel, out_shapes, scratch=(), **specs):
    single = not isinstance(out_shapes, (list, tuple))
    shapes = [out_shapes] if single else list(out_shapes)
    run = pl.pallas_call(
        kernel,
        out_shape=tuple(shapes) if not single else shapes[0],
        scratch_shapes=list(scratch),
        compiler_params=pltpu.CompilerParams(vmem_limit_bytes=24 * 1024 * 1024),
        **specs,
    )
    return run


def shape(*dims, dtype=F32):
    return jax.ShapeDtypeStruct(dims, dtype)


def shift(value, axis, steps):
    count = lax.axis_size(axis)
    return lax.ppermute(value, axis, [(i, (i + steps) % count) for i in range(count)])


def on_device(
    pressure, accumulation, trans_x, trans_y, trans_z, source, well_cells, well_rates, basis, coarse_off, coarse_diag
):
    wo, wz, to_next_y, to_prev_y, coarse = call(
        pack_kernel,
        [shape(576, 128), shape(576, 128), shape(96, 128), shape(88, 128), shape(32, 128)],
        [
            pltpu.VMEM((6, 576, 32), BF16),
            pltpu.VMEM((8, 32, 128), F32),
            pltpu.VMEM((8, 32, 128), F32),
            pltpu.VMEM((26, 1, 4, 32), F32),
            pltpu.VMEM((1, 4, 32), F32),
            pltpu.SemaphoreType.DMA((5,)),
        ],
        in_specs=[pl.BlockSpec(memory_space=pltpu.HBM)] * 5,
    )(
        *(
            pltpu.with_memory_space_constraint(operand, pltpu.HBM)
            for operand in (basis.reshape(6, 576, 32), pressure, trans_y, coarse_off, coarse_diag)
        )
    )
    from_prev_y = shift(to_next_y, "gy", 1)
    from_next_y = shift(to_prev_y, "gy", -1)
    facing = shift(wz, "gz", 1)
    facing_p = shift(pressure, "gz", 1)
    facing_t = shift(trans_z, "gz", 1)
    wz, to_next_x, to_prev_x, strips = call(
        relay_kernel, [shape(576, 128), shape(368, 128), shape(336, 128), shape(48, 128)]
    )(wo, wz, facing, pressure, trans_x, coarse, from_prev_y, from_next_y)
    from_prev_x = shift(to_next_x, "gx", 1)
    from_next_x = shift(to_prev_x, "gx", -1)
    facing_y = shift(strips, "gz", 1)

    corners, up, down = call(collect_kernel, [shape(32, 128), shape(224, 128, dtype=BF16), shape(224, 128, dtype=BF16)])(
        from_prev_x, from_next_x, to_next_x
    )
    facing_x = shift(corners, "gz", 1)
    wells = call(wells_kernel, shape(256, 128))(well_cells.reshape(8, 128), well_rates.reshape(8, 128))
    partial = call(local_kernel, shape(8, 32, 128))(
        pressure, accumulation, trans_x, trans_y, trans_z, source, wells, facing_p, facing_t, from_prev_y, from_next_y
    )
    residual, field, sums_o, sums_z = call(
        sums_kernel, [shape(8, 32, 128), shape(320, 128), shape(48, 128), shape(48, 128)]
    )(partial, pressure, trans_x, wo, wz, from_prev_x, from_next_x, from_prev_y, from_next_y, facing_y)
    count = lax.axis_size("gx") * lax.axis_size("gy")
    message, corners = call(
        tail_kernel,
        [shape(5 * count, 128), shape(32, 128)],
        [pltpu.VMEM((48, 128), F32), pltpu.VMEM((48, 128), F32), pltpu.VMEM((40, 128), F32)],
    )(field, sums_o, sums_z, corners, facing_x)
    shared = lax.all_to_all(message.reshape(count, 1, 640), ("gx", "gy"), 0, 0)
    shared = shared.reshape(5 * count, 128)

    near = call(window_kernel, shape(688, 128))(
        shift(up, "gx", 3), shift(down, "gx", -3), from_prev_x, to_next_x, from_next_x
    )
    coefs = call(stack_kernel, shape(1376, 128))(near, shift(near, "gz", 1))

    own = call(gather_kernel, shape(96, 128), [pltpu.VMEM((26 * 60, 128), F32)])(shared)
    other = shift(own, "gz", 1)
    solution, new_pressure = call(
        solve_kernel,
        [shape(1, 4, 32), shape(8, 32, 128)],
        [
            pltpu.VMEM((96, 128), F32),
            pltpu.VMEM((96, 128), F32),
            pltpu.VMEM((48, 128), F32),
            pltpu.VMEM((320, 128), F32),
        ],
    )(own, other, coefs, wo, wz, from_prev_x, from_next_x, from_prev_y, from_next_y, facing_y, corners, pressure)
    return residual, solution, new_pressure


def solution(mesh):
    cells = P("gx", "gy", "gz")
    in_specs = (
        cells, cells, cells, cells, cells, cells, P(), P(),
        P(None, None, None, "gx", "gy", "gz"), P(None, "gx", "gy", "gz"), cells,
    )

    return jax.shard_map(on_device, mesh=mesh, in_specs=in_specs, out_specs=(cells, cells, cells), check_vma=False)
```

```python
import jax
import jax.numpy as jnp
from jax import lax
from jax.experimental import pallas as pl
from jax.experimental.pallas import tpu as pltpu
from jax.sharding import PartitionSpec as P


damping = 0.8
F32 = jnp.float32
BF16 = jnp.bfloat16


def iota(shape, dim):
    return lax.broadcasted_iota(jnp.int32, shape, dim)


def parts(a):
    high = a.astype(BF16)
    rest = a - high.astype(F32)
    middle = rest.astype(BF16)
    low = (rest - middle.astype(F32)).astype(BF16)
    return high, middle, low


NN = (((1,), (0,)), ((), ()))
NT = (((1,), (1,)), ((), ()))


def dot(a, b, dims=NN):
    return lax.dot_general(a, b, dims, preferred_element_type=F32)


def dot3(a, b, dims=NN):
    high, middle, low = parts(a)
    return dot(high, b, dims) + dot(middle, b, dims) + dot(low, b, dims)


def spread(core):
    lane = iota((128, 128), 0)
    block = iota((128, 128), 1)
    block = jnp.where(block < 64, block, 32 - core)
    own = core * 32 + lane // 4
    inside = jnp.where(block == own, 1.0, 0.0).astype(BF16)
    below = (lane % 4 == 0) & (block == own - 1)
    above = (lane % 4 == 3) & (block == own + 1)
    return inside, jnp.where(below | above, 1.0, 0.0).astype(BF16)


def faced(core, mine, theirs):
    lane = iota(mine.shape, 1)
    return mine + jnp.where(lane == 127 - 127 * core, pltpu.roll(theirs, 126 + core, 1), 0.0)


def pack_kernel(
    basis_in, pressure_in, trans_y_in, coarse_off_in, coarse_diag_in, wo, wz, to_next_y, to_prev_y, coarse,
    basis, pressure, trans_y, coarse_off, coarse_diag, done,
):
    copies = [
        pltpu.make_async_copy(source, target, done.at[n])
        for n, (source, target) in enumerate(
            (
                (basis_in, basis),
                (coarse_off_in, coarse_off),
                (coarse_diag_in, coarse_diag),
                (pressure_in, pressure),
                (trans_y_in, trans_y),
            )
        )
    ]
    for copy in copies:
        copy.start()
    core = lax.axis_index("gz")
    block = iota((32, 128), 0)
    lane = iota((32, 128), 1)

    def place(mask):
        return jnp.where(mask, 1.0, 0.0).astype(BF16)

    for copy in copies:
        copy.wait()
    total = dot(basis[1], place(lane == 4 * block))
    for k in (2, 3, 4):
        total = total + dot(basis[k], place(lane == 4 * block + (k - 1)))
    wo[...] = total
    wz[...] = dot(basis[5], place((lane == 4 * block + 4) | ((block == 31) & (lane == 1) & (core == 0)))) + dot(
        basis[0], place((lane == 4 * block - 1) | ((block == 0) & (lane == 1) & (core == 1)))
    )
    for n in range(2):
        for half, w in enumerate((wo, wz)):
            spot = (2 * n + half) * 12
            to_next_y[pl.ds(spot, 12), :] = w[pl.ds((10 + n) * 48 + 3, 12, stride=4), :]
            to_prev_y[pl.ds(spot, 12), :] = w[pl.ds(n * 48, 12, stride=4), :]
    for x in range(8):
        to_next_y[pl.ds(48 + x, 1), :] = pressure[x, pl.ds(31, 1), :]
        to_next_y[pl.ds(56 + x, 1), :] = trans_y[x, pl.ds(31, 1), :]
        to_prev_y[pl.ds(48 + x, 1), :] = pressure[x, pl.ds(0, 1), :]
    inverse = damping / coarse_diag[0]
    total = jnp.zeros((26, 128), F32)
    line = jnp.zeros((1, 128), F32)
    for by in range(4):
        spot = place(lane == 32 * by + block)
        scale = inverse[by : by + 1]
        total = total + dot3(coarse_off[:, 0, by, :] * scale, spot)
        line = line + dot3(jnp.broadcast_to(scale, (8, 32)), spot)[0:1]
    coarse[...] = jnp.zeros_like(coarse)
    coarse[pl.ds(0, 26), :] = total
    coarse[pl.ds(26, 1), :] = line
    to_next_y[pl.ds(64, 32), :] = coarse[...]
    to_prev_y[pl.ds(56, 32), :] = coarse[...]


def relay_kernel(
    wo, wz, facing, partial, pressure, trans_x, coarse, from_prev_y, from_next_y,
    whole, near_next, near_prev, to_next_x, to_prev_x, strips,
):
    core = lax.axis_index("gz")
    near_next[pl.ds(0, 32), :] = pressure[7]
    near_next[pl.ds(32, 32), :] = trans_x[7]
    near_next[pl.ds(64, 32), :] = partial[6]
    near_next[pl.ds(96, 32), :] = partial[7]
    near_prev[pl.ds(0, 32), :] = pressure[0]
    near_prev[pl.ds(32, 32), :] = partial[0]
    near_prev[pl.ds(64, 32), :] = partial[1]
    whole[...] = faced(core, wz[...], facing[...])
    for j in range(12):
        for half, w in enumerate((wo, whole)):
            to_next_x[pl.ds(96 * half + 8 * j, 8), :] = w[pl.ds(48 * j + 40, 8), :]
            to_prev_x[pl.ds(96 * half + 8 * j, 8), :] = w[pl.ds(48 * j, 8), :]
    for side, strip in enumerate((from_prev_y, from_next_y)):
        for n in range(2):
            strips[pl.ds(side * 24 + n * 12, 12), :] = strip[pl.ds((2 * n + 1) * 12, 12), :]
        for spot in range(4):
            to_next_x[pl.ds(192 + side * 8 + spot * 2, 2), :] = strip[pl.ds(spot * 12 + 10, 2), :]
            to_prev_x[pl.ds(192 + side * 8 + spot * 2, 2), :] = strip[pl.ds(spot * 12, 2), :]
    for ref in (to_next_x, to_prev_x):
        ref[pl.ds(208, 32), :] = from_prev_y[pl.ds(64, 32), :]
        ref[pl.ds(240, 32), :] = coarse[...]
        ref[pl.ds(272, 32), :] = from_next_y[pl.ds(56, 32), :]


def collect_kernel(from_prev_x, from_next_x, own, corners, up, down):
    corners[pl.ds(0, 16), :] = from_prev_x[pl.ds(192, 16), :]
    corners[pl.ds(16, 16), :] = from_next_x[pl.ds(192, 16), :]
    at = iota((96, 128), 0) % 32

    def narrow(rows):
        rest = rows - rows.astype(BF16).astype(F32)
        return jnp.where(at == 27, pltpu.roll(rest, 1, 0), rows).astype(BF16)

    for ref, far, near in ((up, from_prev_x, from_next_x), (down, from_next_x, from_prev_x)):
        outer = narrow(far[pl.ds(208, 96), :]).astype(F32)
        inverses = [outer[32 * yc + 24 : 32 * yc + 32] for yc in range(3)]
        ref[pl.ds(0, 32), :] = jnp.concatenate(inverses + [jnp.zeros((8, 128), F32)], axis=0).astype(BF16)
        ref[pl.ds(32, 96), :] = narrow(own[pl.ds(208, 96), :])
        ref[pl.ds(128, 96), :] = narrow(near[pl.ds(208, 96), :])


def window_kernel(up, down, from_prev_x, own, from_next_x, near):
    def wide(rows):
        rows = rows.astype(F32)
        at = iota(rows.shape, 0) % 32
        return rows + jnp.where(at == 26, pltpu.roll(rows, rows.shape[0] - 1, 0), 0.0)

    for spot, ref in ((0, up), (680, down)):
        near[pl.ds(spot, 8), :] = jnp.zeros((8, 128), F32)
        outer = ref[pl.ds(0, 32), :].astype(F32)
        for yc in range(3):
            near[pl.ds(spot + yc, 1), :] = outer[8 * yc + 2 : 8 * yc + 3] + outer[8 * yc + 3 : 8 * yc + 4]
    near[pl.ds(8, 96), :] = wide(up[pl.ds(32, 96), :])
    near[pl.ds(104, 96), :] = wide(up[pl.ds(128, 96), :])
    near[pl.ds(200, 96), :] = from_prev_x[pl.ds(208, 96), :]
    near[pl.ds(296, 96), :] = own[pl.ds(208, 96), :]
    near[pl.ds(392, 96), :] = from_next_x[pl.ds(208, 96), :]
    near[pl.ds(488, 96), :] = wide(down[pl.ds(128, 96), :])
    near[pl.ds(584, 96), :] = wide(down[pl.ds(32, 96), :])


def stack_kernel(near, far, coefs):
    core = lax.axis_index("gz")
    coefs[pl.ds(pl.multiple_of(core * 688, 8), 688), :] = near[...]
    coefs[pl.ds(pl.multiple_of((1 - core) * 688, 8), 688), :] = far[...]


def wells_kernel(cells, rates, wells):
    gx = lax.axis_index("gx")
    gy = lax.axis_index("gy")
    core = lax.axis_index("gz")
    rows_at = iota((256, 128), 0)
    lane_at = iota((128, 128), 0)
    total = jnp.zeros((256, 128), F32)
    for c in range(8):
        cell = cells[pl.ds(c, 1), :]
        at_x = (cell >> 16) - gx * 8
        at_y = ((cell >> 8) & 255) - gy * 32
        at_z = (cell & 255) - core * 128
        inside = (at_x >= 0) & (at_x < 8) & (at_y >= 0) & (at_y < 32)
        row = jnp.where(inside, at_x * 32 + at_y, -1)
        hit = jnp.where(row == rows_at, 1.0, 0.0).astype(BF16)
        here = at_z == lane_at
        for part in parts(rates[pl.ds(c, 1), :]):
            total = total + dot(hit, jnp.where(here, part.astype(F32), 0.0).astype(BF16), NT)
    wells[...] = total


def local_kernel(
    pressure, accumulation, trans_x, trans_y, trans_z, source, wells, facing_p, facing_t, from_prev_y, from_next_y, partial
):
    gy = lax.axis_index("gy")
    core = lax.axis_index("gz")
    size_y = lax.axis_size("gy")
    row = iota((32, 128), 0)
    lane = iota((32, 128), 1)
    has_next_y = jnp.where(gy < size_y - 1, 1.0, 0.0)
    has_prev_y = jnp.where(gy > 0, 1.0, 0.0)
    has_next_z = jnp.where(core == 0, 1.0, 0.0)
    has_prev_z = jnp.where(core == 1, 1.0, 0.0)
    for x in range(8):
        here = pressure[x]
        flux = jnp.zeros((32, 128), F32)
        if x < 7:
            flux = flux + trans_x[x] * (here - pressure[x + 1])
        if x > 0:
            flux = flux + trans_x[x - 1] * (here - pressure[x - 1])
        after = jnp.where(row == 31, from_next_y[pl.ds(48 + x, 1), :] * has_next_y, pltpu.roll(here, 31, 0))
        before = jnp.where(row == 0, from_prev_y[pl.ds(48 + x, 1), :] * has_prev_y, pltpu.roll(here, 1, 0))
        t_here = trans_y[x]
        t_before = jnp.where(row == 0, from_prev_y[pl.ds(56 + x, 1), :] * has_prev_y, pltpu.roll(t_here, 1, 0))
        flux = flux + t_here * (here - after) + t_before * (here - before)
        other = facing_p[x]
        after = jnp.where(lane == 127, pltpu.roll(other, 127, 1) * has_next_z, pltpu.roll(here, 127, 1))
        before = jnp.where(lane == 0, pltpu.roll(other, 1, 1) * has_prev_z, pltpu.roll(here, 1, 1))
        t_here = trans_z[x]
        t_before = jnp.where(lane == 0, pltpu.roll(facing_t[x], 1, 1) * has_prev_z, pltpu.roll(t_here, 1, 1))
        flux = flux + t_here * (here - after) + t_before * (here - before)
        partial[x] = source[x] + wells[pl.ds(32 * x, 32), :] - accumulation[x] * here - flux


def sums_kernel(
    partial, pressure, trans_x, wo, wz, near_from_prev, near_from_next, from_prev_y, from_next_y, facing_y,
    residual, message, field, sums_o, sums_z,
):
    gx = lax.axis_index("gx")
    core = lax.axis_index("gz")
    size_x = lax.axis_size("gx")
    has_next_x = jnp.where(gx < size_x - 1, 1.0, 0.0)
    has_prev_x = jnp.where(gx > 0, 1.0, 0.0)
    p_prev = near_from_prev[pl.ds(0, 32), :] * has_prev_x
    t_prev = near_from_prev[pl.ds(32, 32), :] * has_prev_x
    p_next = near_from_next[pl.ds(0, 32), :] * has_next_x
    flux_prev = t_prev * (pressure[0] - p_prev)
    flux_next = trans_x[7] * (pressure[7] - p_next)
    planes = [
        near_from_prev[pl.ds(64, 32), :] * has_prev_x,
        near_from_prev[pl.ds(96, 32), :] * has_prev_x + flux_prev * has_prev_x,
    ]
    for x in range(8):
        value = partial[x]
        if x == 0:
            value = value - flux_prev
        if x == 7:
            value = value - flux_next
        residual[x] = value
        planes.append(value)
    planes.append(near_from_next[pl.ds(32, 32), :] * has_next_x + flux_next * has_next_x)
    planes.append(near_from_next[pl.ds(64, 32), :] * has_next_x)
    field[...] = jnp.zeros_like(field)
    for i, plane in enumerate(planes):
        field[pl.ds(40 * i + 2, 32), :] = plane

    sums_o[...] = jnp.zeros_like(sums_o)
    sums_z[...] = jnp.zeros_like(sums_z)
    for by in range(4):
        totals = [None, None]
        for i in range(12):
            upper = field[pl.ds(40 * i + 8 * by, 8), :]
            lower = field[pl.ds(40 * i + 8 * by + 8, 4), :]
            for half, w in enumerate((wo, wz)):
                terms = (
                    w[pl.ds(4 * i + by, 8, stride=48), :] * upper,
                    w[pl.ds(4 * i + by + 384, 4, stride=48), :] * lower,
                )
                old = totals[half]
                totals[half] = terms if old is None else (old[0] + terms[0], old[1] + terms[1])
        for half, sums in enumerate((sums_o, sums_z)):
            a8, a4 = totals[half]
            sums[pl.ds(by + 1, 1), :] = jnp.sum(a8, axis=0, keepdims=True) + jnp.sum(a4, axis=0, keepdims=True)
    for side, (by, first_row, strip) in enumerate(((-1, 2, from_prev_y), (4, 32, from_next_y))):
        for half, sums in enumerate((sums_o, sums_z)):
            total = None
            for n in range(2):
                tile = strip[pl.ds((2 * n + half) * 12, 12), :]
                if half:
                    tile = faced(core, tile, facing_y[pl.ds(side * 24 + n * 12, 12), :])
                line = tile * field[pl.ds(first_row + n, 12, stride=40), :]
                total = line if total is None else total + line
            sums[pl.ds(by + 1, 1), :] = jnp.sum(total, axis=0, keepdims=True)
    inside, reach = spread(core)
    out = dot3(sums_o[...], inside) + dot3(sums_z[...], reach)
    group = iota((1, 128), 1) // 32
    lines = [out[n : n + 1] for n in range(6)]
    row = iota((8, 128), 0)
    mask = (iota((8, 128), 1) == 64 + row) & (row < 6)
    across = jnp.sum(jnp.where(mask, out, 0.0), axis=0, keepdims=True)
    halves = []
    for zc in range(2):
        total = jnp.zeros((1, 128), F32)
        ends = across
        for by in range(4):
            shift = (by * 32 - zc * 32) % 128
            total = jnp.where(group == by, pltpu.roll(lines[by + 1], shift, 1) if shift else lines[by + 1], total)
        for n, line in ((0, lines[5]), (1, lines[0])):
            shift = (n * 32 - zc * 32) % 128
            ends = jnp.where(group == n, pltpu.roll(line, shift, 1) if shift else line, ends)
        halves.append((total, ends))
    first = core == 0
    own = jnp.where(first, halves[0][0], halves[1][0])
    ends = jnp.where(first, halves[0][1], halves[1][1])
    block = jnp.where(row % 2 == 0, own, ends)
    for n in range(message.shape[0] // 8):
        message[pl.ds(8 * n, 8), :] = block


def gather_kernel(shared, own, padded):
    gx = lax.axis_index("gx")
    gy = lax.axis_index("gy")
    core = lax.axis_index("gz")
    size_x = lax.axis_size("gx")
    padded[...] = jnp.zeros_like(padded)
    for x in range(size_x):
        padded[pl.ds((x + 4) * 24 + 4, 16), :] = shared[pl.ds(x * 16, 16), :]
    lane = iota((9, 128), 1)
    source = iota((128, 128), 0)
    target = iota((128, 128), 1)
    at = target // 32
    hit = target % 32 == 31 * core

    def place(mask):
        return jnp.where(mask, 1.0, 0.0).astype(BF16)

    within = place(hit & (source == 65 + at))
    lower = place(hit & (at == 0) & (source == 69))
    upper = place(hit & (at == 3) & (source == 64))

    def line(dy, kind):
        return padded[pl.ds((gx * 12 + gy + 2 + dy) * 2 + kind, 9, stride=24), :]

    ends = [line(dy, 1) for dy in range(-2, 3)]
    own[...] = jnp.zeros_like(own)
    for yc in range(3):
        extra = jnp.where(lane >= 96, pltpu.roll(ends[yc + 2], 64, 1), 0.0)
        own[pl.ds(16 * yc, 9), :] = line(yc - 1, 0) + jnp.where(lane < 32, ends[yc], extra)
        own[pl.ds(48 + 16 * yc, 9), :] = (
            dot3(ends[yc + 1], within) + dot3(ends[yc], lower) + dot3(ends[yc + 2], upper)
        )


OFFSETS = tuple(
    (a, b, c) for a in (-1, 0, 1) for b in (-1, 0, 1) for c in (-1, 0, 1) if (a, b, c) != (0, 0, 0)
)


def solve_kernel(
    own, other, coefs, wo, wz, from_prev_x, from_next_x, from_prev_y, from_next_y, facing_y, tips, facing_x, pressure,
    solution, new_pressure, start, state, blocks, field, corners,
):
    gx = lax.axis_index("gx")
    gy = lax.axis_index("gy")
    core = lax.axis_index("gz")
    size_x = lax.axis_size("gx")
    size_y = lax.axis_size("gy")

    tip = iota((32, 128), 0)
    corners[...] = jnp.where((tip % 8) // 2 % 2 == 1, faced(core, tips[...], facing_x[...]), tips[...])
    at_x = iota((9, 128), 0) + gx - 4
    valid_x = (at_x >= 0) & (at_x < size_x)
    for yc in range(3):
        mine = own[pl.ds(16 * yc, 9), :] + other[pl.ds(48 + 16 * yc, 9), :]
        theirs = other[pl.ds(16 * yc, 9), :] + own[pl.ds(48 + 16 * yc, 9), :]
        valid = valid_x & (gy + yc - 1 >= 0) & (gy + yc - 1 < size_y)
        for zc in range(2):
            spot = (yc * 2 + zc) * 16
            base = zc * 688
            state[pl.ds(spot, 1), :] = coefs[pl.ds(base + yc, 1), :]
            state[pl.ds(spot + 1, 7), :] = coefs[pl.ds(base + 8 + yc * 32 + 26, 7, stride=96), :]
            state[pl.ds(spot + 8, 1), :] = coefs[pl.ds(base + 680 + yc, 1), :]
            value = jnp.where(core == zc, mine, theirs) * state[pl.ds(spot, 9), :]
            value = jnp.where(valid, value, 0.0)
            start[pl.ds(spot, 9), :] = value
            state[pl.ds(spot, 9), :] = value

    lane = iota((7, 128), 1)
    deep = lane % 32
    at_x = iota((7, 128), 0) + gx - 3
    valid_x = (at_x >= 0) & (at_x < size_x)
    for _ in range(3):
        totals = {}
        for yc in range(3):
            for zc in range(2):
                spot = (yc * 2 + zc) * 16 + 1
                totals[yc, zc] = (1.0 - damping) * state[pl.ds(spot, 7), :] + start[pl.ds(spot, 7), :]
        for a in (-1, 0, 1):
            shifted = {}
            for yc in range(3):
                low = state[pl.ds((yc * 2) * 16 + 1 + a, 7), :]
                high = state[pl.ds((yc * 2 + 1) * 16 + 1 + a, 7), :]
                shifted[yc, 0, 0] = low
                shifted[yc, 1, 0] = high
                shifted[yc, 0, 1] = jnp.where(deep == 31, pltpu.roll(high, 31, 1), pltpu.roll(low, 127, 1))
                shifted[yc, 1, 1] = jnp.where(deep == 31, 0.0, pltpu.roll(high, 127, 1))
                shifted[yc, 0, -1] = jnp.where(deep == 0, 0.0, pltpu.roll(low, 1, 1))
                shifted[yc, 1, -1] = jnp.where(deep == 0, pltpu.roll(low, 97, 1), pltpu.roll(high, 1, 1))
            for c in (-1, 0, 1):
                for zc in range(2):
                    up = [pltpu.roll(shifted[yc, zc, c], 96, 1) for yc in range(3)]
                    down = [pltpu.roll(shifted[yc, zc, c], 32, 1) for yc in range(3)]
                    zero = jnp.zeros((7, 128), F32)
                    for yc in range(3):
                        beyond = up[yc + 1] if yc < 2 else zero
                        behind = down[yc - 1] if yc > 0 else zero
                        values = {
                            -1: jnp.where(lane < 32, behind, down[yc]),
                            0: shifted[yc, zc, c],
                            1: jnp.where(lane >= 96, beyond, up[yc]),
                        }
                        for b in (-1, 0, 1):
                            if (a, b, c) == (0, 0, 0):
                                continue
                            number = OFFSETS.index((a, b, c))
                            coef = coefs[pl.ds(zc * 688 + 8 + yc * 32 + number, 7, stride=96), :]
                            totals[yc, zc] = totals[yc, zc] - coef * values[b]
        for yc in range(3):
            valid = valid_x & (gy + yc - 1 >= 0) & (gy + yc - 1 < size_y)
            for zc in range(2):
                state[pl.ds((yc * 2 + zc) * 16 + 1, 7), :] = jnp.where(valid, totals[yc, zc], 0.0)

    low = state[pl.ds(2 * 16 + 4, 1), :]
    high = state[pl.ds(3 * 16 + 4, 1), :]
    mine = jnp.where(core == 0, low, high)
    for by in range(4):
        moved = pltpu.roll(mine, (128 - 32 * by) % 128, 1) if by else mine
        solution[0, pl.ds(by, 1), :] = moved[:, 0:32]

    lane3 = iota((3, 128), 1)
    blocks[...] = jnp.zeros_like(blocks)
    for by in range(-1, 5):
        yc, at = (0, 3) if by < 0 else ((2, 0) if by > 3 else (1, by))
        low = state[pl.ds((yc * 2) * 16 + 3, 3), :]
        high = state[pl.ds((yc * 2 + 1) * 16 + 3, 3), :]
        low = pltpu.roll(low, (128 - 32 * at) % 128, 1) if at else low
        shift = (32 - 32 * at) % 128
        high = pltpu.roll(high, shift, 1) if shift else high
        blocks[pl.ds((by + 1) * 8, 3), :] = jnp.where(lane3 < 32, low, jnp.where(lane3 < 64, high, 0.0))
    inside, reach = spread(core)
    over_o = dot3(blocks[...], inside, NT)
    over_z = dot3(blocks[...], reach, NT)

    def factor(by, column):
        spot = (by + 1) * 8 + column
        return over_o[spot : spot + 1], over_z[spot : spot + 1]

    field[...] = jnp.zeros_like(field)
    for x in range(8):
        entries = [(None, 0, 0, 48, (x + 2) * 4, 1)]
        if x < 2:
            entries.append((from_prev_x, 0, 96, 8, x * 4, 0))
        if x >= 6:
            entries.append((from_next_x, 0, 96, 8, (x - 6) * 4, 2))
        carry = None
        for by in range(4):
            total8 = total4 = None
            for ref, base_o, base_z, step, begin, column in entries:
                factors = factor(by, column)
                for half in range(2):
                    w = ref if ref is not None else (wo, wz)[half]
                    first = (base_o, base_z)[half] + begin + by
                    term8 = w[pl.ds(first, 8, stride=step), :] * factors[half]
                    term4 = w[pl.ds(first + 8 * step, 4, stride=step), :] * factors[half]
                    total8 = term8 if total8 is None else total8 + term8
                    total4 = term4 if total4 is None else total4 + term4
            field[pl.ds(40 * x + 8 * by, 8), :] = total8
            if carry is not None:
                field[pl.ds(40 * x + 8 * by, 4), :] = total8[0:4] + carry
            carry = total4
        field[pl.ds(40 * x + 32, 4), :] = carry
    for side, (by, first_row, strip) in enumerate(((-1, 2, from_prev_y), (4, 32, from_next_y))):
        for n in range(2):
            middle = strip[pl.ds(2 * n * 12 + 2, 8), :] * factor(by, 1)[0]
            tile = faced(core, strip[pl.ds((2 * n + 1) * 12 + 2, 8), :], facing_y[pl.ds(side * 24 + n * 12 + 2, 8), :])
            middle = middle + tile * factor(by, 1)[1]
            rows = pl.ds(first_row + n, 8, stride=40)
            field[rows, :] = field[rows, :] + middle
            for column, first_x in ((0, 0), (2, 6)):
                spot = column * 8 + side * 8 + n * 4
                factors = factor(by, column)
                rows = pl.ds(40 * first_x + first_row + n, 2, stride=40)
                field[rows, :] = (
                    field[rows, :]
                    + corners[pl.ds(spot, 2), :] * factors[0]
                    + corners[pl.ds(spot + 2, 2), :] * factors[1]
                )
    for x in range(8):
        new_pressure[x] = pressure[x] + field[pl.ds(40 * x + 2, 32), :]


def call(kernel, out_shapes, scratch=(), **specs):
    single = not isinstance(out_shapes, (list, tuple))
    shapes = [out_shapes] if single else list(out_shapes)
    run = pl.pallas_call(
        kernel,
        out_shape=tuple(shapes) if not single else shapes[0],
        scratch_shapes=list(scratch),
        compiler_params=pltpu.CompilerParams(vmem_limit_bytes=24 * 1024 * 1024),
        **specs,
    )
    return run


def shape(*dims, dtype=F32):
    return jax.ShapeDtypeStruct(dims, dtype)


def shift(value, axis, steps):
    count = lax.axis_size(axis)
    return lax.ppermute(value, axis, [(i, (i + steps) % count) for i in range(count)])


def on_device(
    pressure, accumulation, trans_x, trans_y, trans_z, source, well_cells, well_rates, basis, coarse_off, coarse_diag
):
    wo, wz, to_next_y, to_prev_y, coarse = call(
        pack_kernel,
        [shape(576, 128), shape(576, 128), shape(96, 128), shape(88, 128), shape(32, 128)],
        [
            pltpu.VMEM((6, 576, 32), BF16),
            pltpu.VMEM((8, 32, 128), F32),
            pltpu.VMEM((8, 32, 128), F32),
            pltpu.VMEM((26, 1, 4, 32), F32),
            pltpu.VMEM((1, 4, 32), F32),
            pltpu.SemaphoreType.DMA((5,)),
        ],
        in_specs=[pl.BlockSpec(memory_space=pltpu.HBM)] * 5,
    )(
        *(
            pltpu.with_memory_space_constraint(operand, pltpu.HBM)
            for operand in (basis.reshape(6, 576, 32), pressure, trans_y, coarse_off, coarse_diag)
        )
    )
    from_prev_y = shift(to_next_y, "gy", 1)
    from_next_y = shift(to_prev_y, "gy", -1)
    facing = shift(wz, "gz", 1)
    facing_p = shift(pressure, "gz", 1)
    facing_t = shift(trans_z, "gz", 1)
    wells = call(wells_kernel, shape(256, 128))(well_cells.reshape(8, 128), well_rates.reshape(8, 128))
    partial = call(local_kernel, shape(8, 32, 128))(
        pressure, accumulation, trans_x, trans_y, trans_z, source, wells, facing_p, facing_t, from_prev_y, from_next_y
    )
    wz, near_next, near_prev, to_next_x, to_prev_x, strips = call(
        relay_kernel,
        [shape(576, 128), shape(128, 128), shape(96, 128), shape(304, 128), shape(304, 128), shape(48, 128)],
    )(wo, wz, facing, partial, pressure, trans_x, coarse, from_prev_y, from_next_y)
    near_from_prev = shift(near_next, "gx", 1)
    near_from_next = shift(near_prev, "gx", -1)
    facing_y = shift(strips, "gz", 1)
    from_prev_x = shift(to_next_x, "gx", 1)
    from_next_x = shift(to_prev_x, "gx", -1)

    count = lax.axis_size("gx") * lax.axis_size("gy")
    residual, message = call(
        sums_kernel,
        [shape(8, 32, 128), shape(2 * count, 128)],
        [pltpu.VMEM((480, 128), F32), pltpu.VMEM((8, 128), F32), pltpu.VMEM((8, 128), F32)],
    )(partial, pressure, trans_x, wo, wz, near_from_prev, near_from_next, from_prev_y, from_next_y, facing_y)
    shared = lax.all_to_all(message.reshape(count, 1, 256), ("gx", "gy"), 0, 0)
    shared = shared.reshape(2 * count, 128)

    tips, up, down = call(
        collect_kernel, [shape(32, 128), shape(224, 128, dtype=BF16), shape(224, 128, dtype=BF16)]
    )(from_prev_x, from_next_x, to_next_x)
    facing_x = shift(tips, "gz", 1)
    near = call(window_kernel, shape(688, 128))(
        shift(up, "gx", 3), shift(down, "gx", -3), from_prev_x, to_next_x, from_next_x
    )
    coefs = call(stack_kernel, shape(1376, 128))(near, shift(near, "gz", 1))

    own = call(gather_kernel, shape(96, 128), [pltpu.VMEM((576, 128), F32)])(shared)
    other = shift(own, "gz", 1)
    solution, new_pressure = call(
        solve_kernel,
        [shape(1, 4, 32), shape(8, 32, 128)],
        [
            pltpu.VMEM((96, 128), F32),
            pltpu.VMEM((96, 128), F32),
            pltpu.VMEM((48, 128), F32),
            pltpu.VMEM((320, 128), F32),
            pltpu.VMEM((32, 128), F32),
        ],
    )(own, other, coefs, wo, wz, from_prev_x, from_next_x, from_prev_y, from_next_y, facing_y, tips, facing_x, pressure)
    return residual, solution, new_pressure


def solution(mesh):
    cells = P("gx", "gy", "gz")
    in_specs = (
        cells, cells, cells, cells, cells, cells, P(), P(),
        P(None, None, None, "gx", "gy", "gz"), P(None, "gx", "gy", "gz"), cells,
    )

    return jax.shard_map(on_device, mesh=mesh, in_specs=in_specs, out_specs=(cells, cells, cells), check_vma=False)
```

```python
import jax
import jax.numpy as jnp
from jax import lax
from jax.experimental import pallas as pl
from jax.experimental.pallas import tpu as pltpu
from jax.sharding import PartitionSpec as P


damping = 0.8
F32 = jnp.float32
BF16 = jnp.bfloat16


def iota(shape, dim):
    return lax.broadcasted_iota(jnp.int32, shape, dim)


def parts(a):
    high = a.astype(BF16)
    rest = a - high.astype(F32)
    middle = rest.astype(BF16)
    low = (rest - middle.astype(F32)).astype(BF16)
    return high, middle, low


NN = (((1,), (0,)), ((), ()))
NT = (((1,), (1,)), ((), ()))


def dot(a, b, dims=NN):
    return lax.dot_general(a, b, dims, preferred_element_type=F32)


def dot3(a, b, dims=NN):
    high, middle, low = parts(a)
    return dot(high, b, dims) + dot(middle, b, dims) + dot(low, b, dims)


def spread(core):
    lane = iota((128, 128), 0)
    block = iota((128, 128), 1)
    block = jnp.where(block < 64, block, 32 - core)
    own = core * 32 + lane // 4
    inside = jnp.where(block == own, 1.0, 0.0).astype(BF16)
    below = (lane % 4 == 0) & (block == own - 1)
    above = (lane % 4 == 3) & (block == own + 1)
    return inside, jnp.where(below | above, 1.0, 0.0).astype(BF16)


def faced(core, mine, theirs):
    lane = iota(mine.shape, 1)
    return mine + jnp.where(lane == 127 - 127 * core, pltpu.roll(theirs, 126 + core, 1), 0.0)


def pack_kernel(
    basis_in, pressure_in, trans_y_in, coarse_off_in, coarse_diag_in, wo, wz, to_next_y, to_prev_y, coarse,
    basis, pressure, trans_y, coarse_off, coarse_diag, done,
):
    def copy(n, source, target):
        return pltpu.make_async_copy(source, target, done.at[n])

    small = (copy(0, coarse_off_in, coarse_off), copy(1, coarse_diag_in, coarse_diag))
    tiles = copy(2, basis_in, basis)
    fields = (copy(3, pressure_in, pressure), copy(4, trans_y_in, trans_y))
    for each in (*small, tiles, *fields):
        each.start()
    core = lax.axis_index("gz")
    block = iota((32, 128), 0)
    lane = iota((32, 128), 1)

    def place(mask):
        return jnp.where(mask, 1.0, 0.0).astype(BF16)

    for each in small:
        each.wait()
    inverse = damping / coarse_diag[0]
    total = jnp.zeros((26, 128), F32)
    line = jnp.zeros((1, 128), F32)
    for by in range(4):
        spot = place(lane == 32 * by + block)
        scale = inverse[by : by + 1]
        total = total + dot3(coarse_off[:, 0, by, :] * scale, spot)
        line = line + dot3(jnp.broadcast_to(scale, (8, 32)), spot)[0:1]
    coarse[...] = jnp.zeros_like(coarse)
    coarse[pl.ds(0, 26), :] = total
    coarse[pl.ds(26, 1), :] = line
    tiles.wait()
    reach = dot(basis[0], place((lane == 4 * block - 1) | ((block == 0) & (lane == 1) & (core == 1))))
    total = dot(basis[1], place(lane == 4 * block))
    for k in (2, 3, 4):
        total = total + dot(basis[k], place(lane == 4 * block + (k - 1)))
    wo[...] = total
    wz[...] = reach + dot(basis[5], place((lane == 4 * block + 4) | ((block == 31) & (lane == 1) & (core == 0))))
    for each in fields:
        each.wait()
    for n in range(2):
        for half, w in enumerate((wo, wz)):
            spot = (2 * n + half) * 12
            to_next_y[pl.ds(spot, 12), :] = w[pl.ds((10 + n) * 48 + 3, 12, stride=4), :]
            to_prev_y[pl.ds(spot, 12), :] = w[pl.ds(n * 48, 12, stride=4), :]
    for x in range(8):
        to_next_y[pl.ds(48 + x, 1), :] = pressure[x, pl.ds(31, 1), :]
        to_next_y[pl.ds(56 + x, 1), :] = trans_y[x, pl.ds(31, 1), :]
        to_prev_y[pl.ds(48 + x, 1), :] = pressure[x, pl.ds(0, 1), :]
    to_next_y[pl.ds(64, 32), :] = coarse[...]
    to_prev_y[pl.ds(56, 32), :] = coarse[...]


def relay_kernel(
    wo, wz, facing, partial, pressure, trans_x, coarse, from_prev_y, from_next_y,
    whole, near_next, near_prev, to_next_x, to_prev_x, strips,
):
    core = lax.axis_index("gz")
    near_next[pl.ds(0, 32), :] = pressure[7]
    near_next[pl.ds(32, 32), :] = trans_x[7]
    near_next[pl.ds(64, 32), :] = partial[6]
    near_next[pl.ds(96, 32), :] = partial[7]
    near_prev[pl.ds(0, 32), :] = pressure[0]
    near_prev[pl.ds(32, 32), :] = partial[0]
    near_prev[pl.ds(64, 32), :] = partial[1]
    whole[...] = faced(core, wz[...], facing[...])
    for j in range(12):
        for half, w in enumerate((wo, whole)):
            to_next_x[pl.ds(96 * half + 8 * j, 8), :] = w[pl.ds(48 * j + 40, 8), :]
            to_prev_x[pl.ds(96 * half + 8 * j, 8), :] = w[pl.ds(48 * j, 8), :]
    for side, strip in enumerate((from_prev_y, from_next_y)):
        for n in range(2):
            strips[pl.ds(side * 24 + n * 12, 12), :] = strip[pl.ds((2 * n + 1) * 12, 12), :]
        for spot in range(4):
            to_next_x[pl.ds(192 + side * 8 + spot * 2, 2), :] = strip[pl.ds(spot * 12 + 10, 2), :]
            to_prev_x[pl.ds(192 + side * 8 + spot * 2, 2), :] = strip[pl.ds(spot * 12, 2), :]
    for ref in (to_next_x, to_prev_x):
        ref[pl.ds(208, 32), :] = from_prev_y[pl.ds(64, 32), :]
        ref[pl.ds(240, 32), :] = coarse[...]
        ref[pl.ds(272, 32), :] = from_next_y[pl.ds(56, 32), :]


def collect_kernel(from_prev_x, from_next_x, own, corners, up, down):
    corners[pl.ds(0, 16), :] = from_prev_x[pl.ds(192, 16), :]
    corners[pl.ds(16, 16), :] = from_next_x[pl.ds(192, 16), :]
    at = iota((96, 128), 0) % 32

    def narrow(rows):
        rest = rows - rows.astype(BF16).astype(F32)
        return jnp.where(at == 27, pltpu.roll(rest, 1, 0), rows).astype(BF16)

    for ref, far, near in ((up, from_prev_x, from_next_x), (down, from_next_x, from_prev_x)):
        outer = narrow(far[pl.ds(208, 96), :]).astype(F32)
        inverses = [outer[32 * yc + 24 : 32 * yc + 32] for yc in range(3)]
        ref[pl.ds(0, 32), :] = jnp.concatenate(inverses + [jnp.zeros((8, 128), F32)], axis=0).astype(BF16)
        ref[pl.ds(32, 96), :] = narrow(own[pl.ds(208, 96), :])
        ref[pl.ds(128, 96), :] = narrow(near[pl.ds(208, 96), :])


def window_kernel(up, down, from_prev_x, own, from_next_x, near, rows):
    def wide(rows):
        rows = rows.astype(F32)
        at = iota(rows.shape, 0) % 32
        return rows + jnp.where(at == 26, pltpu.roll(rows, rows.shape[0] - 1, 0), 0.0)

    rows[pl.ds(0, 96), :] = wide(up[pl.ds(32, 96), :])
    rows[pl.ds(96, 96), :] = wide(up[pl.ds(128, 96), :])
    rows[pl.ds(192, 96), :] = from_prev_x[pl.ds(208, 96), :]
    rows[pl.ds(288, 96), :] = own[pl.ds(208, 96), :]
    rows[pl.ds(384, 96), :] = from_next_x[pl.ds(208, 96), :]
    rows[pl.ds(480, 96), :] = wide(down[pl.ds(128, 96), :])
    rows[pl.ds(576, 96), :] = wide(down[pl.ds(32, 96), :])
    for yc in range(3):
        for number in range(26):
            near[pl.ds((yc * 26 + number) * 8, 7), :] = rows[pl.ds(yc * 32 + number, 7, stride=96), :]
            near[pl.ds((yc * 26 + number) * 8 + 7, 1), :] = jnp.zeros((1, 128), F32)
        spot = 624 + 16 * yc
        near[pl.ds(spot + 8, 8), :] = jnp.zeros((8, 128), F32)
        near[pl.ds(spot + 1, 7), :] = rows[pl.ds(yc * 32 + 26, 7, stride=96), :]
        for at, ref in ((0, up), (8, down)):
            outer = ref[pl.ds(0, 32), :].astype(F32)
            near[pl.ds(spot + at, 1), :] = outer[8 * yc + 2 : 8 * yc + 3] + outer[8 * yc + 3 : 8 * yc + 4]


def stack_kernel(near, far, coefs):
    core = lax.axis_index("gz")
    coefs[pl.ds(pl.multiple_of(core * 672, 8), 672), :] = near[...]
    coefs[pl.ds(pl.multiple_of((1 - core) * 672, 8), 672), :] = far[...]


def wells_kernel(cells, rates, wells):
    gx = lax.axis_index("gx")
    gy = lax.axis_index("gy")
    core = lax.axis_index("gz")
    rows_at = iota((256, 128), 0)
    lane_at = iota((128, 128), 0)
    total = jnp.zeros((256, 128), F32)
    for c in range(8):
        cell = cells[pl.ds(c, 1), :]
        at_x = (cell >> 16) - gx * 8
        at_y = ((cell >> 8) & 255) - gy * 32
        at_z = (cell & 255) - core * 128
        inside = (at_x >= 0) & (at_x < 8) & (at_y >= 0) & (at_y < 32)
        row = jnp.where(inside, at_x * 32 + at_y, -1)
        hit = jnp.where(row == rows_at, 1.0, 0.0).astype(BF16)
        here = at_z == lane_at
        for part in parts(rates[pl.ds(c, 1), :]):
            total = total + dot(hit, jnp.where(here, part.astype(F32), 0.0).astype(BF16), NT)
    wells[...] = total


def local_kernel(
    pressure, accumulation, trans_x, trans_y, trans_z, source, wells, facing_p, facing_t, from_prev_y, from_next_y, partial
):
    gy = lax.axis_index("gy")
    core = lax.axis_index("gz")
    size_y = lax.axis_size("gy")
    row = iota((32, 128), 0)
    lane = iota((32, 128), 1)
    has_next_y = jnp.where(gy < size_y - 1, 1.0, 0.0)
    has_prev_y = jnp.where(gy > 0, 1.0, 0.0)
    has_next_z = jnp.where(core == 0, 1.0, 0.0)
    has_prev_z = jnp.where(core == 1, 1.0, 0.0)
    for x in range(8):
        here = pressure[x]
        flux = jnp.zeros((32, 128), F32)
        if x < 7:
            flux = flux + trans_x[x] * (here - pressure[x + 1])
        if x > 0:
            flux = flux + trans_x[x - 1] * (here - pressure[x - 1])
        after = jnp.where(row == 31, from_next_y[pl.ds(48 + x, 1), :] * has_next_y, pltpu.roll(here, 31, 0))
        before = jnp.where(row == 0, from_prev_y[pl.ds(48 + x, 1), :] * has_prev_y, pltpu.roll(here, 1, 0))
        t_here = trans_y[x]
        t_before = jnp.where(row == 0, from_prev_y[pl.ds(56 + x, 1), :] * has_prev_y, pltpu.roll(t_here, 1, 0))
        flux = flux + t_here * (here - after) + t_before * (here - before)
        other = facing_p[x]
        after = jnp.where(lane == 127, pltpu.roll(other, 127, 1) * has_next_z, pltpu.roll(here, 127, 1))
        before = jnp.where(lane == 0, pltpu.roll(other, 1, 1) * has_prev_z, pltpu.roll(here, 1, 1))
        t_here = trans_z[x]
        t_before = jnp.where(lane == 0, pltpu.roll(facing_t[x], 1, 1) * has_prev_z, pltpu.roll(t_here, 1, 1))
        flux = flux + t_here * (here - after) + t_before * (here - before)
        partial[x] = source[x] + wells[pl.ds(32 * x, 32), :] - accumulation[x] * here - flux


def sums_kernel(
    partial, pressure, trans_x, wo, wz, near_from_prev, near_from_next, from_prev_y, from_next_y, facing_y,
    residual, message, field, sums_o, sums_z,
):
    gx = lax.axis_index("gx")
    core = lax.axis_index("gz")
    size_x = lax.axis_size("gx")
    has_next_x = jnp.where(gx < size_x - 1, 1.0, 0.0)
    has_prev_x = jnp.where(gx > 0, 1.0, 0.0)
    p_prev = near_from_prev[pl.ds(0, 32), :] * has_prev_x
    t_prev = near_from_prev[pl.ds(32, 32), :] * has_prev_x
    p_next = near_from_next[pl.ds(0, 32), :] * has_next_x
    flux_prev = t_prev * (pressure[0] - p_prev)
    flux_next = trans_x[7] * (pressure[7] - p_next)
    planes = [
        near_from_prev[pl.ds(64, 32), :] * has_prev_x,
        near_from_prev[pl.ds(96, 32), :] * has_prev_x + flux_prev * has_prev_x,
    ]
    for x in range(8):
        value = partial[x]
        if x == 0:
            value = value - flux_prev
        if x == 7:
            value = value - flux_next
        residual[x] = value
        planes.append(value)
    planes.append(near_from_next[pl.ds(32, 32), :] * has_next_x + flux_next * has_next_x)
    planes.append(near_from_next[pl.ds(64, 32), :] * has_next_x)
    field[...] = jnp.zeros_like(field)
    for i, plane in enumerate(planes):
        field[pl.ds(40 * i + 2, 32), :] = plane

    sums_o[...] = jnp.zeros_like(sums_o)
    sums_z[...] = jnp.zeros_like(sums_z)
    for by in range(4):
        totals = [None, None]
        for i in range(12):
            upper = field[pl.ds(40 * i + 8 * by, 8), :]
            lower = field[pl.ds(40 * i + 8 * by + 8, 4), :]
            for half, w in enumerate((wo, wz)):
                terms = (
                    w[pl.ds(4 * i + by, 8, stride=48), :] * upper,
                    w[pl.ds(4 * i + by + 384, 4, stride=48), :] * lower,
                )
                old = totals[half]
                totals[half] = terms if old is None else (old[0] + terms[0], old[1] + terms[1])
        for half, sums in enumerate((sums_o, sums_z)):
            a8, a4 = totals[half]
            sums[pl.ds(by + 1, 1), :] = jnp.sum(a8, axis=0, keepdims=True) + jnp.sum(a4, axis=0, keepdims=True)
    for side, (by, first_row, strip) in enumerate(((-1, 2, from_prev_y), (4, 32, from_next_y))):
        for half, sums in enumerate((sums_o, sums_z)):
            total = None
            for n in range(2):
                tile = strip[pl.ds((2 * n + half) * 12, 12), :]
                if half:
                    tile = faced(core, tile, facing_y[pl.ds(side * 24 + n * 12, 12), :])
                line = tile * field[pl.ds(first_row + n, 12, stride=40), :]
                total = line if total is None else total + line
            sums[pl.ds(by + 1, 1), :] = jnp.sum(total, axis=0, keepdims=True)
    inside, reach = spread(core)
    out = dot3(sums_o[...], inside) + dot3(sums_z[...], reach)
    group = iota((1, 128), 1) // 32
    lines = [out[n : n + 1] for n in range(6)]
    row = iota((8, 128), 0)
    mask = (iota((8, 128), 1) == 64 + row) & (row < 6)
    across = jnp.sum(jnp.where(mask, out, 0.0), axis=0, keepdims=True)
    halves = []
    for zc in range(2):
        total = jnp.zeros((1, 128), F32)
        ends = across
        for by in range(4):
            shift = (by * 32 - zc * 32) % 128
            total = jnp.where(group == by, pltpu.roll(lines[by + 1], shift, 1) if shift else lines[by + 1], total)
        for n, line in ((0, lines[5]), (1, lines[0])):
            shift = (n * 32 - zc * 32) % 128
            ends = jnp.where(group == n, pltpu.roll(line, shift, 1) if shift else line, ends)
        halves.append((total, ends))
    first = core == 0
    own = jnp.where(first, halves[0][0], halves[1][0])
    ends = jnp.where(first, halves[0][1], halves[1][1])
    block = jnp.where(row % 2 == 0, own, ends)
    for n in range(message.shape[0] // 8):
        message[pl.ds(8 * n, 8), :] = block


def gather_kernel(shared, own, padded):
    gx = lax.axis_index("gx")
    gy = lax.axis_index("gy")
    core = lax.axis_index("gz")
    size_x = lax.axis_size("gx")
    padded[...] = jnp.zeros_like(padded)
    for x in range(size_x):
        padded[pl.ds((x + 4) * 24 + 4, 16), :] = shared[pl.ds(x * 16, 16), :]
    lane = iota((9, 128), 1)
    source = iota((128, 128), 0)
    target = iota((128, 128), 1)
    at = target // 32
    hit = target % 32 == 31 * core

    def place(mask):
        return jnp.where(mask, 1.0, 0.0).astype(BF16)

    within = place(hit & (source == 65 + at))
    lower = place(hit & (at == 0) & (source == 69))
    upper = place(hit & (at == 3) & (source == 64))

    def line(dy, kind):
        return padded[pl.ds((gx * 12 + gy + 2 + dy) * 2 + kind, 9, stride=24), :]

    ends = [line(dy, 1) for dy in range(-2, 3)]
    own[...] = jnp.zeros_like(own)
    for yc in range(3):
        extra = jnp.where(lane >= 96, pltpu.roll(ends[yc + 2], 64, 1), 0.0)
        own[pl.ds(16 * yc, 9), :] = line(yc - 1, 0) + jnp.where(lane < 32, ends[yc], extra)
        own[pl.ds(48 + 16 * yc, 9), :] = (
            dot3(ends[yc + 1], within) + dot3(ends[yc], lower) + dot3(ends[yc + 2], upper)
        )


OFFSETS = tuple(
    (a, b, c) for a in (-1, 0, 1) for b in (-1, 0, 1) for c in (-1, 0, 1) if (a, b, c) != (0, 0, 0)
)


def solve_kernel(
    own, other, coefs, wo, wz, from_prev_x, from_next_x, from_prev_y, from_next_y, facing_y, tips, facing_x, pressure,
    solution, new_pressure, start, state, blocks, field, corners,
):
    gx = lax.axis_index("gx")
    gy = lax.axis_index("gy")
    core = lax.axis_index("gz")
    size_x = lax.axis_size("gx")
    size_y = lax.axis_size("gy")

    tip = iota((32, 128), 0)
    corners[...] = jnp.where((tip % 8) // 2 % 2 == 1, faced(core, tips[...], facing_x[...]), tips[...])
    at_x = iota((9, 128), 0) + gx - 4
    valid_x = (at_x >= 0) & (at_x < size_x)
    for yc in range(3):
        mine = own[pl.ds(16 * yc, 9), :] + other[pl.ds(48 + 16 * yc, 9), :]
        theirs = other[pl.ds(16 * yc, 9), :] + own[pl.ds(48 + 16 * yc, 9), :]
        valid = valid_x & (gy + yc - 1 >= 0) & (gy + yc - 1 < size_y)
        for zc in range(2):
            spot = (yc * 2 + zc) * 16
            value = jnp.where(core == zc, mine, theirs) * coefs[pl.ds(zc * 672 + 624 + 16 * yc, 9), :]
            value = jnp.where(valid, value, 0.0)
            start[pl.ds(spot, 9), :] = value
            state[pl.ds(spot, 9), :] = value

    lane = iota((7, 128), 1)
    deep = lane % 32
    at_x = iota((7, 128), 0) + gx - 3
    valid_x = (at_x >= 0) & (at_x < size_x)
    for _ in range(3):
        totals = {}
        for yc in range(3):
            for zc in range(2):
                spot = (yc * 2 + zc) * 16 + 1
                totals[yc, zc] = (1.0 - damping) * state[pl.ds(spot, 7), :] + start[pl.ds(spot, 7), :]
        for a in (-1, 0, 1):
            shifted = {}
            for yc in range(3):
                low = state[pl.ds((yc * 2) * 16 + 1 + a, 7), :]
                high = state[pl.ds((yc * 2 + 1) * 16 + 1 + a, 7), :]
                shifted[yc, 0, 0] = low
                shifted[yc, 1, 0] = high
                shifted[yc, 0, 1] = jnp.where(deep == 31, pltpu.roll(high, 31, 1), pltpu.roll(low, 127, 1))
                shifted[yc, 1, 1] = jnp.where(deep == 31, 0.0, pltpu.roll(high, 127, 1))
                shifted[yc, 0, -1] = jnp.where(deep == 0, 0.0, pltpu.roll(low, 1, 1))
                shifted[yc, 1, -1] = jnp.where(deep == 0, pltpu.roll(low, 97, 1), pltpu.roll(high, 1, 1))
            for c in (-1, 0, 1):
                for zc in range(2):
                    up = [pltpu.roll(shifted[yc, zc, c], 96, 1) for yc in range(3)]
                    down = [pltpu.roll(shifted[yc, zc, c], 32, 1) for yc in range(3)]
                    zero = jnp.zeros((7, 128), F32)
                    for yc in range(3):
                        beyond = up[yc + 1] if yc < 2 else zero
                        behind = down[yc - 1] if yc > 0 else zero
                        values = {
                            -1: jnp.where(lane < 32, behind, down[yc]),
                            0: shifted[yc, zc, c],
                            1: jnp.where(lane >= 96, beyond, up[yc]),
                        }
                        for b in (-1, 0, 1):
                            if (a, b, c) == (0, 0, 0):
                                continue
                            number = OFFSETS.index((a, b, c))
                            coef = coefs[pl.ds(zc * 672 + (yc * 26 + number) * 8, 7), :]
                            totals[yc, zc] = totals[yc, zc] - coef * values[b]
        for yc in range(3):
            valid = valid_x & (gy + yc - 1 >= 0) & (gy + yc - 1 < size_y)
            for zc in range(2):
                state[pl.ds((yc * 2 + zc) * 16 + 1, 7), :] = jnp.where(valid, totals[yc, zc], 0.0)

    low = state[pl.ds(2 * 16 + 4, 1), :]
    high = state[pl.ds(3 * 16 + 4, 1), :]
    mine = jnp.where(core == 0, low, high)
    for by in range(4):
        moved = pltpu.roll(mine, (128 - 32 * by) % 128, 1) if by else mine
        solution[0, pl.ds(by, 1), :] = moved[:, 0:32]

    lane3 = iota((3, 128), 1)
    blocks[...] = jnp.zeros_like(blocks)
    for by in range(-1, 5):
        yc, at = (0, 3) if by < 0 else ((2, 0) if by > 3 else (1, by))
        low = state[pl.ds((yc * 2) * 16 + 3, 3), :]
        high = state[pl.ds((yc * 2 + 1) * 16 + 3, 3), :]
        low = pltpu.roll(low, (128 - 32 * at) % 128, 1) if at else low
        shift = (32 - 32 * at) % 128
        high = pltpu.roll(high, shift, 1) if shift else high
        blocks[pl.ds((by + 1) * 8, 3), :] = jnp.where(lane3 < 32, low, jnp.where(lane3 < 64, high, 0.0))
    inside, reach = spread(core)
    over_o = dot3(blocks[...], inside, NT)
    over_z = dot3(blocks[...], reach, NT)

    def factor(by, column):
        spot = (by + 1) * 8 + column
        return over_o[spot : spot + 1], over_z[spot : spot + 1]

    field[...] = jnp.zeros_like(field)
    for x in range(8):
        entries = [(None, 0, 0, 48, (x + 2) * 4, 1)]
        if x < 2:
            entries.append((from_prev_x, 0, 96, 8, x * 4, 0))
        if x >= 6:
            entries.append((from_next_x, 0, 96, 8, (x - 6) * 4, 2))
        carry = None
        for by in range(4):
            total8 = total4 = None
            for ref, base_o, base_z, step, begin, column in entries:
                factors = factor(by, column)
                for half in range(2):
                    w = ref if ref is not None else (wo, wz)[half]
                    first = (base_o, base_z)[half] + begin + by
                    term8 = w[pl.ds(first, 8, stride=step), :] * factors[half]
                    term4 = w[pl.ds(first + 8 * step, 4, stride=step), :] * factors[half]
                    total8 = term8 if total8 is None else total8 + term8
                    total4 = term4 if total4 is None else total4 + term4
            field[pl.ds(40 * x + 8 * by, 8), :] = total8
            if carry is not None:
                field[pl.ds(40 * x + 8 * by, 4), :] = total8[0:4] + carry
            carry = total4
        field[pl.ds(40 * x + 32, 4), :] = carry
    for side, (by, first_row, strip) in enumerate(((-1, 2, from_prev_y), (4, 32, from_next_y))):
        for n in range(2):
            middle = strip[pl.ds(2 * n * 12 + 2, 8), :] * factor(by, 1)[0]
            tile = faced(core, strip[pl.ds((2 * n + 1) * 12 + 2, 8), :], facing_y[pl.ds(side * 24 + n * 12 + 2, 8), :])
            middle = middle + tile * factor(by, 1)[1]
            rows = pl.ds(first_row + n, 8, stride=40)
            field[rows, :] = field[rows, :] + middle
            for column, first_x in ((0, 0), (2, 6)):
                spot = column * 8 + side * 8 + n * 4
                factors = factor(by, column)
                rows = pl.ds(40 * first_x + first_row + n, 2, stride=40)
                field[rows, :] = (
                    field[rows, :]
                    + corners[pl.ds(spot, 2), :] * factors[0]
                    + corners[pl.ds(spot + 2, 2), :] * factors[1]
                )
    for x in range(8):
        new_pressure[x] = pressure[x] + field[pl.ds(40 * x + 2, 32), :]


def call(kernel, out_shapes, scratch=(), **specs):
    single = not isinstance(out_shapes, (list, tuple))
    shapes = [out_shapes] if single else list(out_shapes)
    run = pl.pallas_call(
        kernel,
        out_shape=tuple(shapes) if not single else shapes[0],
        scratch_shapes=list(scratch),
        compiler_params=pltpu.CompilerParams(vmem_limit_bytes=24 * 1024 * 1024),
        **specs,
    )
    return run


def shape(*dims, dtype=F32):
    return jax.ShapeDtypeStruct(dims, dtype)


def shift(value, axis, steps):
    count = lax.axis_size(axis)
    return lax.ppermute(value, axis, [(i, (i + steps) % count) for i in range(count)])


def on_device(
    pressure, accumulation, trans_x, trans_y, trans_z, source, well_cells, well_rates, basis, coarse_off, coarse_diag
):
    wo, wz, to_next_y, to_prev_y, coarse = call(
        pack_kernel,
        [shape(576, 128), shape(576, 128), shape(96, 128), shape(88, 128), shape(32, 128)],
        [
            pltpu.VMEM((6, 576, 32), BF16),
            pltpu.VMEM((8, 32, 128), F32),
            pltpu.VMEM((8, 32, 128), F32),
            pltpu.VMEM((26, 1, 4, 32), F32),
            pltpu.VMEM((1, 4, 32), F32),
            pltpu.SemaphoreType.DMA((5,)),
        ],
        in_specs=[pl.BlockSpec(memory_space=pltpu.HBM)] * 5,
    )(
        *(
            pltpu.with_memory_space_constraint(operand, pltpu.HBM)
            for operand in (basis.reshape(6, 576, 32), pressure, trans_y, coarse_off, coarse_diag)
        )
    )
    from_prev_y = shift(to_next_y, "gy", 1)
    from_next_y = shift(to_prev_y, "gy", -1)
    facing = shift(wz, "gz", 1)
    facing_p = shift(pressure, "gz", 1)
    facing_t = shift(trans_z, "gz", 1)
    wells = call(wells_kernel, shape(256, 128))(well_cells.reshape(8, 128), well_rates.reshape(8, 128))
    partial = call(local_kernel, shape(8, 32, 128))(
        pressure, accumulation, trans_x, trans_y, trans_z, source, wells, facing_p, facing_t, from_prev_y, from_next_y
    )
    wz, near_next, near_prev, to_next_x, to_prev_x, strips = call(
        relay_kernel,
        [shape(576, 128), shape(128, 128), shape(96, 128), shape(304, 128), shape(304, 128), shape(48, 128)],
    )(wo, wz, facing, partial, pressure, trans_x, coarse, from_prev_y, from_next_y)
    near_from_prev = shift(near_next, "gx", 1)
    near_from_next = shift(near_prev, "gx", -1)
    facing_y = shift(strips, "gz", 1)
    from_prev_x = shift(to_next_x, "gx", 1)
    from_next_x = shift(to_prev_x, "gx", -1)

    count = lax.axis_size("gx") * lax.axis_size("gy")
    residual, message = call(
        sums_kernel,
        [shape(8, 32, 128), shape(2 * count, 128)],
        [pltpu.VMEM((480, 128), F32), pltpu.VMEM((8, 128), F32), pltpu.VMEM((8, 128), F32)],
    )(partial, pressure, trans_x, wo, wz, near_from_prev, near_from_next, from_prev_y, from_next_y, facing_y)
    shared = lax.all_to_all(message.reshape(count, 1, 256), ("gx", "gy"), 0, 0)
    shared = shared.reshape(2 * count, 128)
    tips, up, down = call(
        collect_kernel, [shape(32, 128), shape(224, 128, dtype=BF16), shape(224, 128, dtype=BF16)]
    )(from_prev_x, from_next_x, to_next_x)
    facing_x = shift(tips, "gz", 1)
    near = call(window_kernel, shape(672, 128), [pltpu.VMEM((672, 128), F32)])(
        shift(up, "gx", 3), shift(down, "gx", -3), from_prev_x, to_next_x, from_next_x
    )
    coefs = call(stack_kernel, shape(1344, 128))(near, shift(near, "gz", 1))

    own = call(gather_kernel, shape(96, 128), [pltpu.VMEM((576, 128), F32)])(shared)
    other = shift(own, "gz", 1)
    solution, new_pressure = call(
        solve_kernel,
        [shape(1, 4, 32), shape(8, 32, 128)],
        [
            pltpu.VMEM((96, 128), F32),
            pltpu.VMEM((96, 128), F32),
            pltpu.VMEM((48, 128), F32),
            pltpu.VMEM((320, 128), F32),
            pltpu.VMEM((32, 128), F32),
        ],
    )(own, other, coefs, wo, wz, from_prev_x, from_next_x, from_prev_y, from_next_y, facing_y, tips, facing_x, pressure)
    return residual, solution, new_pressure


def solution(mesh):
    cells = P("gx", "gy", "gz")
    in_specs = (
        cells, cells, cells, cells, cells, cells, P(), P(),
        P(None, None, None, "gx", "gy", "gz"), P(None, "gx", "gy", "gz"), cells,
    )

    return jax.shard_map(on_device, mesh=mesh, in_specs=in_specs, out_specs=(cells, cells, cells), check_vma=False)
```

```python
import jax
import jax.numpy as jnp
from jax import lax
from jax.experimental import pallas as pl
from jax.experimental.pallas import tpu as pltpu
from jax.sharding import PartitionSpec as P


damping = 0.8
F32 = jnp.float32
BF16 = jnp.bfloat16


def iota(shape, dim):
    return lax.broadcasted_iota(jnp.int32, shape, dim)


def parts(a):
    high = a.astype(BF16)
    rest = a - high.astype(F32)
    middle = rest.astype(BF16)
    low = (rest - middle.astype(F32)).astype(BF16)
    return high, middle, low


NN = (((1,), (0,)), ((), ()))
NT = (((1,), (1,)), ((), ()))


def dot(a, b, dims=NN):
    return lax.dot_general(a, b, dims, preferred_element_type=F32)


def dot3(a, b, dims=NN):
    high, middle, low = parts(a)
    return dot(high, b, dims) + dot(middle, b, dims) + dot(low, b, dims)


def spread(core):
    lane = iota((128, 128), 0)
    block = iota((128, 128), 1)
    block = jnp.where(block < 64, block, 32 - core)
    own = core * 32 + lane // 4
    inside = jnp.where(block == own, 1.0, 0.0).astype(BF16)
    below = (lane % 4 == 0) & (block == own - 1)
    above = (lane % 4 == 3) & (block == own + 1)
    return inside, jnp.where(below | above, 1.0, 0.0).astype(BF16)


def faced(core, mine, theirs):
    lane = iota(mine.shape, 1)
    return mine + jnp.where(lane == 127 - 127 * core, pltpu.roll(theirs, 126 + core, 1), 0.0)


def place(mask):
    return jnp.where(mask, 1.0, 0.0).astype(BF16)


def spread_tiles(core, basis):
    block = iota((32, 128), 0)
    lane = iota((32, 128), 1)
    inner = dot(basis[1], place(lane == 4 * block))
    for k in (2, 3, 4):
        inner = inner + dot(basis[k], place(lane == 4 * block + (k - 1)))
    outer = dot(basis[5], place((lane == 4 * block + 4) | ((block == 31) & (lane == 1) & (core == 0)))) + dot(
        basis[0], place((lane == 4 * block - 1) | ((block == 0) & (lane == 1) & (core == 1)))
    )
    return inner, outer


def pack_kernel(basis_in, wo, wz, basis, done):
    copy = pltpu.make_async_copy(basis_in, basis, done)
    copy.start()
    copy.wait()
    inner, outer = spread_tiles(lax.axis_index("gz"), basis)
    wo[...] = inner
    wz[...] = outer


def front_kernel(
    basis_in, pressure_in, trans_y_in, coarse_off_in, coarse_diag_in, to_next_y, to_prev_y, coarse,
    basis, pressure, trans_y, coarse_off, coarse_diag, wo, wz, done,
):
    def copy(n, source, target):
        return pltpu.make_async_copy(source, target, done.at[n])

    small = (copy(0, coarse_off_in, coarse_off), copy(1, coarse_diag_in, coarse_diag))
    large = (
        copy(2, basis_in.at[:, pl.ds(0, 96)], basis.at[:, pl.ds(0, 96)]),
        copy(3, basis_in.at[:, pl.ds(480, 96)], basis.at[:, pl.ds(96, 96)]),
        copy(4, pressure_in, pressure),
        copy(5, trans_y_in, trans_y),
    )
    for each in (*small, *large):
        each.start()
    core = lax.axis_index("gz")
    block = iota((32, 128), 0)
    lane = iota((32, 128), 1)
    for each in small:
        each.wait()
    inverse = damping / coarse_diag[0]
    total = jnp.zeros((26, 128), F32)
    line = jnp.zeros((1, 128), F32)
    for by in range(4):
        spot = place(lane == 32 * by + block)
        scale = inverse[by : by + 1]
        total = total + dot3(coarse_off[:, 0, by, :] * scale, spot)
        line = line + dot3(jnp.broadcast_to(scale, (8, 32)), spot)[0:1]
    coarse[...] = jnp.zeros_like(coarse)
    coarse[pl.ds(0, 26), :] = total
    coarse[pl.ds(26, 1), :] = line
    for each in large:
        each.wait()
    inner, outer = spread_tiles(core, basis)
    wo[...] = inner
    wz[...] = outer
    for n in range(2):
        for half, w in enumerate((wo, wz)):
            spot = (2 * n + half) * 12
            to_next_y[pl.ds(spot, 12), :] = w[pl.ds((2 + n) * 48 + 3, 12, stride=4), :]
            to_prev_y[pl.ds(spot, 12), :] = w[pl.ds(n * 48, 12, stride=4), :]
    for x in range(8):
        to_next_y[pl.ds(48 + x, 1), :] = pressure[x, pl.ds(31, 1), :]
        to_next_y[pl.ds(56 + x, 1), :] = trans_y[x, pl.ds(31, 1), :]
        to_prev_y[pl.ds(48 + x, 1), :] = pressure[x, pl.ds(0, 1), :]
    to_next_y[pl.ds(64, 32), :] = coarse[...]
    to_prev_y[pl.ds(56, 32), :] = coarse[...]


def relay_kernel(
    wo, wz, facing, partial, pressure, trans_x, coarse, from_prev_y, from_next_y,
    whole, near_next, near_prev, to_next_x, to_prev_x, strips,
):
    core = lax.axis_index("gz")
    near_next[pl.ds(0, 32), :] = pressure[7]
    near_next[pl.ds(32, 32), :] = trans_x[7]
    near_next[pl.ds(64, 32), :] = partial[6]
    near_next[pl.ds(96, 32), :] = partial[7]
    near_prev[pl.ds(0, 32), :] = pressure[0]
    near_prev[pl.ds(32, 32), :] = partial[0]
    near_prev[pl.ds(64, 32), :] = partial[1]
    whole[...] = faced(core, wz[...], facing[...])
    for j in range(12):
        for half, w in enumerate((wo, whole)):
            to_next_x[pl.ds(96 * half + 8 * j, 8), :] = w[pl.ds(48 * j + 40, 8), :]
            to_prev_x[pl.ds(96 * half + 8 * j, 8), :] = w[pl.ds(48 * j, 8), :]
    for side, strip in enumerate((from_prev_y, from_next_y)):
        for n in range(2):
            strips[pl.ds(side * 24 + n * 12, 12), :] = strip[pl.ds((2 * n + 1) * 12, 12), :]
        for spot in range(4):
            to_next_x[pl.ds(192 + side * 8 + spot * 2, 2), :] = strip[pl.ds(spot * 12 + 10, 2), :]
            to_prev_x[pl.ds(192 + side * 8 + spot * 2, 2), :] = strip[pl.ds(spot * 12, 2), :]
    for ref in (to_next_x, to_prev_x):
        ref[pl.ds(208, 32), :] = from_prev_y[pl.ds(64, 32), :]
        ref[pl.ds(240, 32), :] = coarse[...]
        ref[pl.ds(272, 32), :] = from_next_y[pl.ds(56, 32), :]


def collect_kernel(from_prev_x, from_next_x, own, corners, up, down):
    corners[pl.ds(0, 16), :] = from_prev_x[pl.ds(192, 16), :]
    corners[pl.ds(16, 16), :] = from_next_x[pl.ds(192, 16), :]
    at = iota((96, 128), 0) % 32

    def narrow(rows):
        rest = rows - rows.astype(BF16).astype(F32)
        return jnp.where(at == 27, pltpu.roll(rest, 1, 0), rows).astype(BF16)

    for ref, far, near in ((up, from_prev_x, from_next_x), (down, from_next_x, from_prev_x)):
        outer = narrow(far[pl.ds(208, 96), :]).astype(F32)
        inverses = [outer[32 * yc + 24 : 32 * yc + 32] for yc in range(3)]
        ref[pl.ds(0, 32), :] = jnp.concatenate(inverses + [jnp.zeros((8, 128), F32)], axis=0).astype(BF16)
        ref[pl.ds(32, 96), :] = narrow(own[pl.ds(208, 96), :])
        ref[pl.ds(128, 96), :] = narrow(near[pl.ds(208, 96), :])


def window_kernel(up, down, from_prev_x, own, from_next_x, near, rows):
    def wide(rows):
        rows = rows.astype(F32)
        at = iota(rows.shape, 0) % 32
        return rows + jnp.where(at == 26, pltpu.roll(rows, rows.shape[0] - 1, 0), 0.0)

    rows[pl.ds(0, 96), :] = wide(up[pl.ds(32, 96), :])
    rows[pl.ds(96, 96), :] = wide(up[pl.ds(128, 96), :])
    rows[pl.ds(192, 96), :] = from_prev_x[pl.ds(208, 96), :]
    rows[pl.ds(288, 96), :] = own[pl.ds(208, 96), :]
    rows[pl.ds(384, 96), :] = from_next_x[pl.ds(208, 96), :]
    rows[pl.ds(480, 96), :] = wide(down[pl.ds(128, 96), :])
    rows[pl.ds(576, 96), :] = wide(down[pl.ds(32, 96), :])
    for yc in range(3):
        for number in range(26):
            near[pl.ds((yc * 26 + number) * 8, 7), :] = rows[pl.ds(yc * 32 + number, 7, stride=96), :]
            near[pl.ds((yc * 26 + number) * 8 + 7, 1), :] = jnp.zeros((1, 128), F32)
        spot = 624 + 16 * yc
        near[pl.ds(spot + 8, 8), :] = jnp.zeros((8, 128), F32)
        near[pl.ds(spot + 1, 7), :] = rows[pl.ds(yc * 32 + 26, 7, stride=96), :]
        for at, ref in ((0, up), (8, down)):
            outer = ref[pl.ds(0, 32), :].astype(F32)
            near[pl.ds(spot + at, 1), :] = outer[8 * yc + 2 : 8 * yc + 3] + outer[8 * yc + 3 : 8 * yc + 4]


def stack_kernel(near, far, coefs):
    core = lax.axis_index("gz")
    coefs[pl.ds(pl.multiple_of(core * 672, 8), 672), :] = near[...]
    coefs[pl.ds(pl.multiple_of((1 - core) * 672, 8), 672), :] = far[...]


def wells_kernel(cells, rates, wells):
    gx = lax.axis_index("gx")
    gy = lax.axis_index("gy")
    core = lax.axis_index("gz")
    rows_at = iota((256, 128), 0)
    lane_at = iota((128, 128), 0)
    total = jnp.zeros((256, 128), F32)
    for c in range(8):
        cell = cells[pl.ds(c, 1), :]
        at_x = (cell >> 16) - gx * 8
        at_y = ((cell >> 8) & 255) - gy * 32
        at_z = (cell & 255) - core * 128
        inside = (at_x >= 0) & (at_x < 8) & (at_y >= 0) & (at_y < 32)
        row = jnp.where(inside, at_x * 32 + at_y, -1)
        hit = jnp.where(row == rows_at, 1.0, 0.0).astype(BF16)
        here = at_z == lane_at
        for part in parts(rates[pl.ds(c, 1), :]):
            total = total + dot(hit, jnp.where(here, part.astype(F32), 0.0).astype(BF16), NT)
    wells[...] = total


def local_kernel(
    pressure, accumulation, trans_x, trans_y, trans_z, source, wells, facing_p, facing_t, from_prev_y, from_next_y, partial
):
    gy = lax.axis_index("gy")
    core = lax.axis_index("gz")
    size_y = lax.axis_size("gy")
    row = iota((32, 128), 0)
    lane = iota((32, 128), 1)
    has_next_y = jnp.where(gy < size_y - 1, 1.0, 0.0)
    has_prev_y = jnp.where(gy > 0, 1.0, 0.0)
    has_next_z = jnp.where(core == 0, 1.0, 0.0)
    has_prev_z = jnp.where(core == 1, 1.0, 0.0)
    for x in range(8):
        here = pressure[x]
        flux = jnp.zeros((32, 128), F32)
        if x < 7:
            flux = flux + trans_x[x] * (here - pressure[x + 1])
        if x > 0:
            flux = flux + trans_x[x - 1] * (here - pressure[x - 1])
        after = jnp.where(row == 31, from_next_y[pl.ds(48 + x, 1), :] * has_next_y, pltpu.roll(here, 31, 0))
        before = jnp.where(row == 0, from_prev_y[pl.ds(48 + x, 1), :] * has_prev_y, pltpu.roll(here, 1, 0))
        t_here = trans_y[x]
        t_before = jnp.where(row == 0, from_prev_y[pl.ds(56 + x, 1), :] * has_prev_y, pltpu.roll(t_here, 1, 0))
        flux = flux + t_here * (here - after) + t_before * (here - before)
        other = facing_p[x]
        after = jnp.where(lane == 127, pltpu.roll(other, 127, 1) * has_next_z, pltpu.roll(here, 127, 1))
        before = jnp.where(lane == 0, pltpu.roll(other, 1, 1) * has_prev_z, pltpu.roll(here, 1, 1))
        t_here = trans_z[x]
        t_before = jnp.where(lane == 0, pltpu.roll(facing_t[x], 1, 1) * has_prev_z, pltpu.roll(t_here, 1, 1))
        flux = flux + t_here * (here - after) + t_before * (here - before)
        partial[x] = source[x] + wells[pl.ds(32 * x, 32), :] - accumulation[x] * here - flux


def sums_kernel(
    partial, pressure, trans_x, wo, wz, near_from_prev, near_from_next, from_prev_y, from_next_y, facing_y,
    residual, message, field, sums_o, sums_z,
):
    gx = lax.axis_index("gx")
    core = lax.axis_index("gz")
    size_x = lax.axis_size("gx")
    has_next_x = jnp.where(gx < size_x - 1, 1.0, 0.0)
    has_prev_x = jnp.where(gx > 0, 1.0, 0.0)
    p_prev = near_from_prev[pl.ds(0, 32), :] * has_prev_x
    t_prev = near_from_prev[pl.ds(32, 32), :] * has_prev_x
    p_next = near_from_next[pl.ds(0, 32), :] * has_next_x
    flux_prev = t_prev * (pressure[0] - p_prev)
    flux_next = trans_x[7] * (pressure[7] - p_next)
    planes = [
        near_from_prev[pl.ds(64, 32), :] * has_prev_x,
        near_from_prev[pl.ds(96, 32), :] * has_prev_x + flux_prev * has_prev_x,
    ]
    for x in range(8):
        value = partial[x]
        if x == 0:
            value = value - flux_prev
        if x == 7:
            value = value - flux_next
        residual[x] = value
        planes.append(value)
    planes.append(near_from_next[pl.ds(32, 32), :] * has_next_x + flux_next * has_next_x)
    planes.append(near_from_next[pl.ds(64, 32), :] * has_next_x)
    field[...] = jnp.zeros_like(field)
    for i, plane in enumerate(planes):
        field[pl.ds(40 * i + 2, 32), :] = plane

    sums_o[...] = jnp.zeros_like(sums_o)
    sums_z[...] = jnp.zeros_like(sums_z)
    for by in range(4):
        totals = [None, None]
        for i in range(12):
            upper = field[pl.ds(40 * i + 8 * by, 8), :]
            lower = field[pl.ds(40 * i + 8 * by + 8, 4), :]
            for half, w in enumerate((wo, wz)):
                terms = (
                    w[pl.ds(4 * i + by, 8, stride=48), :] * upper,
                    w[pl.ds(4 * i + by + 384, 4, stride=48), :] * lower,
                )
                old = totals[half]
                totals[half] = terms if old is None else (old[0] + terms[0], old[1] + terms[1])
        for half, sums in enumerate((sums_o, sums_z)):
            a8, a4 = totals[half]
            sums[pl.ds(by + 1, 1), :] = jnp.sum(a8, axis=0, keepdims=True) + jnp.sum(a4, axis=0, keepdims=True)
    for side, (by, first_row, strip) in enumerate(((-1, 2, from_prev_y), (4, 32, from_next_y))):
        for half, sums in enumerate((sums_o, sums_z)):
            total = None
            for n in range(2):
                tile = strip[pl.ds((2 * n + half) * 12, 12), :]
                if half:
                    tile = faced(core, tile, facing_y[pl.ds(side * 24 + n * 12, 12), :])
                line = tile * field[pl.ds(first_row + n, 12, stride=40), :]
                total = line if total is None else total + line
            sums[pl.ds(by + 1, 1), :] = jnp.sum(total, axis=0, keepdims=True)
    inside, reach = spread(core)
    out = dot3(sums_o[...], inside) + dot3(sums_z[...], reach)
    group = iota((1, 128), 1) // 32
    lines = [out[n : n + 1] for n in range(6)]
    row = iota((8, 128), 0)
    mask = (iota((8, 128), 1) == 64 + row) & (row < 6)
    across = jnp.sum(jnp.where(mask, out, 0.0), axis=0, keepdims=True)
    halves = []
    for zc in range(2):
        total = jnp.zeros((1, 128), F32)
        ends = across
        for by in range(4):
            shift = (by * 32 - zc * 32) % 128
            total = jnp.where(group == by, pltpu.roll(lines[by + 1], shift, 1) if shift else lines[by + 1], total)
        for n, line in ((0, lines[5]), (1, lines[0])):
            shift = (n * 32 - zc * 32) % 128
            ends = jnp.where(group == n, pltpu.roll(line, shift, 1) if shift else line, ends)
        halves.append((total, ends))
    first = core == 0
    own = jnp.where(first, halves[0][0], halves[1][0])
    ends = jnp.where(first, halves[0][1], halves[1][1])
    block = jnp.where(row % 2 == 0, own, ends)
    for n in range(message.shape[0] // 8):
        message[pl.ds(8 * n, 8), :] = block


def gather_kernel(shared, own, padded):
    gx = lax.axis_index("gx")
    gy = lax.axis_index("gy")
    core = lax.axis_index("gz")
    size_x = lax.axis_size("gx")
    padded[...] = jnp.zeros_like(padded)
    for x in range(size_x):
        padded[pl.ds((x + 4) * 24 + 4, 16), :] = shared[pl.ds(x * 16, 16), :]
    lane = iota((9, 128), 1)
    source = iota((128, 128), 0)
    target = iota((128, 128), 1)
    at = target // 32
    hit = target % 32 == 31 * core

    def place(mask):
        return jnp.where(mask, 1.0, 0.0).astype(BF16)

    within = place(hit & (source == 65 + at))
    lower = place(hit & (at == 0) & (source == 69))
    upper = place(hit & (at == 3) & (source == 64))

    def line(dy, kind):
        return padded[pl.ds((gx * 12 + gy + 2 + dy) * 2 + kind, 9, stride=24), :]

    ends = [line(dy, 1) for dy in range(-2, 3)]
    own[...] = jnp.zeros_like(own)
    for yc in range(3):
        extra = jnp.where(lane >= 96, pltpu.roll(ends[yc + 2], 64, 1), 0.0)
        own[pl.ds(16 * yc, 9), :] = line(yc - 1, 0) + jnp.where(lane < 32, ends[yc], extra)
        own[pl.ds(48 + 16 * yc, 9), :] = (
            dot3(ends[yc + 1], within) + dot3(ends[yc], lower) + dot3(ends[yc + 2], upper)
        )


OFFSETS = tuple(
    (a, b, c) for a in (-1, 0, 1) for b in (-1, 0, 1) for c in (-1, 0, 1) if (a, b, c) != (0, 0, 0)
)


def solve_kernel(
    own, other, coefs, wo, wz, from_prev_x, from_next_x, from_prev_y, from_next_y, facing_y, tips, facing_x, pressure,
    solution, new_pressure, start, state, blocks, field, corners,
):
    gx = lax.axis_index("gx")
    gy = lax.axis_index("gy")
    core = lax.axis_index("gz")
    size_x = lax.axis_size("gx")
    size_y = lax.axis_size("gy")

    tip = iota((32, 128), 0)
    corners[...] = jnp.where((tip % 8) // 2 % 2 == 1, faced(core, tips[...], facing_x[...]), tips[...])
    at_x = iota((9, 128), 0) + gx - 4
    valid_x = (at_x >= 0) & (at_x < size_x)
    for yc in range(3):
        mine = own[pl.ds(16 * yc, 9), :] + other[pl.ds(48 + 16 * yc, 9), :]
        theirs = other[pl.ds(16 * yc, 9), :] + own[pl.ds(48 + 16 * yc, 9), :]
        valid = valid_x & (gy + yc - 1 >= 0) & (gy + yc - 1 < size_y)
        for zc in range(2):
            spot = (yc * 2 + zc) * 16
            value = jnp.where(core == zc, mine, theirs) * coefs[pl.ds(zc * 672 + 624 + 16 * yc, 9), :]
            value = jnp.where(valid, value, 0.0)
            start[pl.ds(spot, 9), :] = value
            state[pl.ds(spot, 9), :] = value

    lane = iota((7, 128), 1)
    deep = lane % 32
    at_x = iota((7, 128), 0) + gx - 3
    valid_x = (at_x >= 0) & (at_x < size_x)
    for _ in range(3):
        totals = {}
        for yc in range(3):
            for zc in range(2):
                spot = (yc * 2 + zc) * 16 + 1
                totals[yc, zc] = (1.0 - damping) * state[pl.ds(spot, 7), :] + start[pl.ds(spot, 7), :]
        for a in (-1, 0, 1):
            shifted = {}
            for yc in range(3):
                low = state[pl.ds((yc * 2) * 16 + 1 + a, 7), :]
                high = state[pl.ds((yc * 2 + 1) * 16 + 1 + a, 7), :]
                shifted[yc, 0, 0] = low
                shifted[yc, 1, 0] = high
                shifted[yc, 0, 1] = jnp.where(deep == 31, pltpu.roll(high, 31, 1), pltpu.roll(low, 127, 1))
                shifted[yc, 1, 1] = jnp.where(deep == 31, 0.0, pltpu.roll(high, 127, 1))
                shifted[yc, 0, -1] = jnp.where(deep == 0, 0.0, pltpu.roll(low, 1, 1))
                shifted[yc, 1, -1] = jnp.where(deep == 0, pltpu.roll(low, 97, 1), pltpu.roll(high, 1, 1))
            for c in (-1, 0, 1):
                for zc in range(2):
                    up = [pltpu.roll(shifted[yc, zc, c], 96, 1) for yc in range(3)]
                    down = [pltpu.roll(shifted[yc, zc, c], 32, 1) for yc in range(3)]
                    zero = jnp.zeros((7, 128), F32)
                    for yc in range(3):
                        beyond = up[yc + 1] if yc < 2 else zero
                        behind = down[yc - 1] if yc > 0 else zero
                        values = {
                            -1: jnp.where(lane < 32, behind, down[yc]),
                            0: shifted[yc, zc, c],
                            1: jnp.where(lane >= 96, beyond, up[yc]),
                        }
                        for b in (-1, 0, 1):
                            if (a, b, c) == (0, 0, 0):
                                continue
                            number = OFFSETS.index((a, b, c))
                            coef = coefs[pl.ds(zc * 672 + (yc * 26 + number) * 8, 7), :]
                            totals[yc, zc] = totals[yc, zc] - coef * values[b]
        for yc in range(3):
            valid = valid_x & (gy + yc - 1 >= 0) & (gy + yc - 1 < size_y)
            for zc in range(2):
                state[pl.ds((yc * 2 + zc) * 16 + 1, 7), :] = jnp.where(valid, totals[yc, zc], 0.0)

    low = state[pl.ds(2 * 16 + 4, 1), :]
    high = state[pl.ds(3 * 16 + 4, 1), :]
    mine = jnp.where(core == 0, low, high)
    for by in range(4):
        moved = pltpu.roll(mine, (128 - 32 * by) % 128, 1) if by else mine
        solution[0, pl.ds(by, 1), :] = moved[:, 0:32]

    lane3 = iota((3, 128), 1)
    blocks[...] = jnp.zeros_like(blocks)
    for by in range(-1, 5):
        yc, at = (0, 3) if by < 0 else ((2, 0) if by > 3 else (1, by))
        low = state[pl.ds((yc * 2) * 16 + 3, 3), :]
        high = state[pl.ds((yc * 2 + 1) * 16 + 3, 3), :]
        low = pltpu.roll(low, (128 - 32 * at) % 128, 1) if at else low
        shift = (32 - 32 * at) % 128
        high = pltpu.roll(high, shift, 1) if shift else high
        blocks[pl.ds((by + 1) * 8, 3), :] = jnp.where(lane3 < 32, low, jnp.where(lane3 < 64, high, 0.0))
    inside, reach = spread(core)
    over_o = dot3(blocks[...], inside, NT)
    over_z = dot3(blocks[...], reach, NT)

    def factor(by, column):
        spot = (by + 1) * 8 + column
        return over_o[spot : spot + 1], over_z[spot : spot + 1]

    field[...] = jnp.zeros_like(field)
    for x in range(8):
        entries = [(None, 0, 0, 48, (x + 2) * 4, 1)]
        if x < 2:
            entries.append((from_prev_x, 0, 96, 8, x * 4, 0))
        if x >= 6:
            entries.append((from_next_x, 0, 96, 8, (x - 6) * 4, 2))
        carry = None
        for by in range(4):
            total8 = total4 = None
            for ref, base_o, base_z, step, begin, column in entries:
                factors = factor(by, column)
                for half in range(2):
                    w = ref if ref is not None else (wo, wz)[half]
                    first = (base_o, base_z)[half] + begin + by
                    term8 = w[pl.ds(first, 8, stride=step), :] * factors[half]
                    term4 = w[pl.ds(first + 8 * step, 4, stride=step), :] * factors[half]
                    total8 = term8 if total8 is None else total8 + term8
                    total4 = term4 if total4 is None else total4 + term4
            field[pl.ds(40 * x + 8 * by, 8), :] = total8
            if carry is not None:
                field[pl.ds(40 * x + 8 * by, 4), :] = total8[0:4] + carry
            carry = total4
        field[pl.ds(40 * x + 32, 4), :] = carry
    for side, (by, first_row, strip) in enumerate(((-1, 2, from_prev_y), (4, 32, from_next_y))):
        for n in range(2):
            middle = strip[pl.ds(2 * n * 12 + 2, 8), :] * factor(by, 1)[0]
            tile = faced(core, strip[pl.ds((2 * n + 1) * 12 + 2, 8), :], facing_y[pl.ds(side * 24 + n * 12 + 2, 8), :])
            middle = middle + tile * factor(by, 1)[1]
            rows = pl.ds(first_row + n, 8, stride=40)
            field[rows, :] = field[rows, :] + middle
            for column, first_x in ((0, 0), (2, 6)):
                spot = column * 8 + side * 8 + n * 4
                factors = factor(by, column)
                rows = pl.ds(40 * first_x + first_row + n, 2, stride=40)
                field[rows, :] = (
                    field[rows, :]
                    + corners[pl.ds(spot, 2), :] * factors[0]
                    + corners[pl.ds(spot + 2, 2), :] * factors[1]
                )
    for x in range(8):
        new_pressure[x] = pressure[x] + field[pl.ds(40 * x + 2, 32), :]


def call(kernel, out_shapes, scratch=(), **specs):
    single = not isinstance(out_shapes, (list, tuple))
    shapes = [out_shapes] if single else list(out_shapes)
    run = pl.pallas_call(
        kernel,
        out_shape=tuple(shapes) if not single else shapes[0],
        scratch_shapes=list(scratch),
        compiler_params=pltpu.CompilerParams(vmem_limit_bytes=24 * 1024 * 1024),
        **specs,
    )
    return run


def shape(*dims, dtype=F32):
    return jax.ShapeDtypeStruct(dims, dtype)


def shift(value, axis, steps):
    count = lax.axis_size(axis)
    return lax.ppermute(value, axis, [(i, (i + steps) % count) for i in range(count)])


def on_device(
    pressure, accumulation, trans_x, trans_y, trans_z, source, well_cells, well_rates, basis, coarse_off, coarse_diag
):
    tiles, *others = (
        pltpu.with_memory_space_constraint(operand, pltpu.HBM)
        for operand in (basis.reshape(6, 576, 32), pressure, trans_y, coarse_off, coarse_diag)
    )
    to_next_y, to_prev_y, coarse = call(
        front_kernel,
        [shape(96, 128), shape(88, 128), shape(32, 128)],
        [
            pltpu.VMEM((6, 192, 32), BF16),
            pltpu.VMEM((8, 32, 128), F32),
            pltpu.VMEM((8, 32, 128), F32),
            pltpu.VMEM((26, 1, 4, 32), F32),
            pltpu.VMEM((1, 4, 32), F32),
            pltpu.VMEM((192, 128), F32),
            pltpu.VMEM((192, 128), F32),
            pltpu.SemaphoreType.DMA((6,)),
        ],
        in_specs=[pl.BlockSpec(memory_space=pltpu.HBM)] * 5,
    )(tiles, *others)
    from_prev_y = shift(to_next_y, "gy", 1)
    from_next_y = shift(to_prev_y, "gy", -1)
    wo, wz = call(
        pack_kernel,
        [shape(576, 128), shape(576, 128)],
        [pltpu.VMEM((6, 576, 32), BF16), pltpu.SemaphoreType.DMA],
        in_specs=[pl.BlockSpec(memory_space=pltpu.HBM)],
    )(tiles)
    facing = shift(wz, "gz", 1)
    facing_p = shift(pressure, "gz", 1)
    facing_t = shift(trans_z, "gz", 1)
    wells = call(wells_kernel, shape(256, 128))(well_cells.reshape(8, 128), well_rates.reshape(8, 128))
    partial = call(local_kernel, shape(8, 32, 128))(
        pressure, accumulation, trans_x, trans_y, trans_z, source, wells, facing_p, facing_t, from_prev_y, from_next_y
    )
    wz, near_next, near_prev, to_next_x, to_prev_x, strips = call(
        relay_kernel,
        [shape(576, 128), shape(128, 128), shape(96, 128), shape(304, 128), shape(304, 128), shape(48, 128)],
    )(wo, wz, facing, partial, pressure, trans_x, coarse, from_prev_y, from_next_y)
    near_from_prev = shift(near_next, "gx", 1)
    near_from_next = shift(near_prev, "gx", -1)
    facing_y = shift(strips, "gz", 1)
    from_prev_x = shift(to_next_x, "gx", 1)
    from_next_x = shift(to_prev_x, "gx", -1)

    count = lax.axis_size("gx") * lax.axis_size("gy")
    residual, message = call(
        sums_kernel,
        [shape(8, 32, 128), shape(2 * count, 128)],
        [pltpu.VMEM((480, 128), F32), pltpu.VMEM((8, 128), F32), pltpu.VMEM((8, 128), F32)],
    )(partial, pressure, trans_x, wo, wz, near_from_prev, near_from_next, from_prev_y, from_next_y, facing_y)
    shared = lax.all_to_all(message.reshape(count, 1, 256), ("gx", "gy"), 0, 0)
    shared = shared.reshape(2 * count, 128)
    tips, up, down = call(
        collect_kernel, [shape(32, 128), shape(224, 128, dtype=BF16), shape(224, 128, dtype=BF16)]
    )(from_prev_x, from_next_x, to_next_x)
    facing_x = shift(tips, "gz", 1)
    near = call(window_kernel, shape(672, 128), [pltpu.VMEM((672, 128), F32)])(
        shift(up, "gx", 3), shift(down, "gx", -3), from_prev_x, to_next_x, from_next_x
    )
    coefs = call(stack_kernel, shape(1344, 128))(near, shift(near, "gz", 1))

    own = call(gather_kernel, shape(96, 128), [pltpu.VMEM((576, 128), F32)])(shared)
    other = shift(own, "gz", 1)
    solution, new_pressure = call(
        solve_kernel,
        [shape(1, 4, 32), shape(8, 32, 128)],
        [
            pltpu.VMEM((96, 128), F32),
            pltpu.VMEM((96, 128), F32),
            pltpu.VMEM((48, 128), F32),
            pltpu.VMEM((320, 128), F32),
            pltpu.VMEM((32, 128), F32),
        ],
    )(own, other, coefs, wo, wz, from_prev_x, from_next_x, from_prev_y, from_next_y, facing_y, tips, facing_x, pressure)
    return residual, solution, new_pressure


def solution(mesh):
    cells = P("gx", "gy", "gz")
    in_specs = (
        cells, cells, cells, cells, cells, cells, P(), P(),
        P(None, None, None, "gx", "gy", "gz"), P(None, "gx", "gy", "gz"), cells,
    )

    return jax.shard_map(on_device, mesh=mesh, in_specs=in_specs, out_specs=(cells, cells, cells), check_vma=False)
```
